512 devices in a mesh: shard: 64 (over x, z, core), tensor: 8 (over y).
Axes of the slice: x: 4, y: 8, z: 8, core: 2. Of those that a mesh axis runs over, the one named last changes fastest.
Arguments:
- grad: float32 [8, 512, 1024], P(None, 'shard', 'tensor'), may hold values from -500 to 500
- momentum: float32 [8, 512, 1024], P(None, 'shard', 'tensor'), may hold values from -6 to 6
- weight: float32 [8, 512, 1024], P(None, 'shard', 'tensor'), may hold values from -0.625 to 0.625
Outputs:
- new_weight: float32 [8, 512, 1024], P(None, 'shard', 'tensor')
- new_momentum: float32 [8, 512, 1024], P(None, 'shard', 'tensor')
- update: float32 [8, 512, 1024], P(None, 'shard', 'tensor')
The draws below stay inside these ranges and needn't reach their ends.
All inputs are finite; a program needn't handle non-finite values.
Results may differ from the reference program's by a relative error of at most 0.0078.
Values may be sent and summed in bfloat16 or wider, within the bound.
A program may use at most 64 MiB of HBM per device.

```python
import math
import jax
import jax.numpy as jnp
from jax import lax

D = 1024
KV = 512
MATS = 8
ITERS = 3
N_TENSOR = 8


def draw_grad(key, part):
    keys = jax.random.split(jax.random.fold_in(key, 7), 3)
    row = jnp.arange(KV, dtype=jnp.float32) / KV
    col = jnp.arange(D)
    block = D // N_TENSOR
    col_ramp = 3.0 ** (col.astype(jnp.float32) / D) * 3.0 ** ((col % block).astype(jnp.float32) / block)
    row_scale = jnp.exp(jax.random.uniform(keys[1], (MATS, KV, 1), jnp.float32, 0.0, math.log(10.0))) * (3.0 ** row)[None, :, None]
    col_scale = jnp.exp(jax.random.uniform(keys[2], (MATS, 1, D), jnp.float32, 0.0, math.log(10.0))) * col_ramp[None, None, :]
    noise = jnp.clip(jax.random.normal(keys[0], (MATS, KV, D), jnp.float32), -4.0, 4.0)
    factor = 0.05
    return jnp.clip(factor * noise * row_scale * col_scale, -500.0, 500.0)


def block_levels(own_key, shape, cuts, least, top_value):
    loudness = 1.0
    for dim, blocks in cuts:
        heights = jax.random.uniform(jax.random.fold_in(jax.random.fold_in(own_key, 6), dim), (blocks,), jnp.float32, least / len(cuts), top_value / len(cuts))
        loudness = loudness * jnp.repeat(jnp.exp(heights), shape[dim] // blocks).reshape((-1,) + (1,) * (len(shape) - 1 - dim))
    return loudness


def centred(rng, shape, deviation, bound, pieces=(), kind=jnp.bfloat16):
    drawn = deviation * jax.random.normal(rng, shape, jnp.float32)
    if pieces:
        drawn = drawn * block_levels(rng, shape, pieces, -0.22, 0.18)
    return jnp.clip(drawn, -bound, bound).astype(kind)


def setup_inputs(seed: int = 0) -> dict:
    streams_of = jax.random.split(jax.random.key(seed), 4)
    grad = draw_grad(jax.random.fold_in(streams_of[3], 71), 0)
    momentum = centred(streams_of[1], (MATS, KV, D), 1.0, 6.0, ((1, 64), (2, 8)), jnp.float32)
    weight = centred(streams_of[2], (MATS, KV, D), 0.04, 0.625, ((1, 64), (2, 8)), jnp.float32)
    return {"grad": grad, "momentum": momentum, "weight": weight}


mu_decay = 0.95
learn_rate = 0.05
weight_decay = 0.1
update_gain = 0.2
first_coef = 3.4445
second_coef = -4.775
third_coef = 2.0315
epsilon = 1e-07

def newton_schulz(start):
    iterate = start
    for step in range(ITERS):
        gram = jnp.dot(iterate, iterate.T, preferred_element_type=jnp.float32)
        poly = second_coef * gram + third_coef * jnp.dot(gram, gram, precision=lax.Precision.HIGHEST)
        wide = iterate.astype(jnp.float32)
        iterate = (first_coef * wide + jnp.dot(poly, wide, precision=lax.Precision.HIGHEST)).astype(jnp.bfloat16)
    return iterate

def reference(grad, momentum, weight):
    new_momentum = mu_decay * momentum + grad
    advance = lax.optimization_barrier((grad + mu_decay * new_momentum).astype(jnp.bfloat16))
    wide = advance.astype(jnp.float32)
    frob = jnp.sqrt(lax.optimization_barrier(jnp.sum(wide * wide, axis=(1, 2), keepdims=True))) + epsilon
    start = (wide / frob).astype(jnp.bfloat16)
    ortho = lax.map(newton_schulz, start)
    update = update_gain * math.sqrt(D) * ortho.astype(jnp.float32)
    new_weight = weight - learn_rate * (update + weight_decay * weight)
    return (new_weight, new_momentum, update)
```

```python
import math

import jax
import jax.numpy as jnp
from jax import lax
from jax.sharding import PartitionSpec as P

ITERS = 3


mu_decay = 0.95
learn_rate = 0.05
weight_decay = 0.1
update_gain = 0.2
first_coef = 3.4445
second_coef = -4.775
third_coef = 2.0315
epsilon = 1e-07


def polish(iterate, gram):
    wide = iterate.astype(jnp.float32)
    squared = jnp.dot(gram, gram, precision=lax.Precision.HIGHEST)
    poly = second_coef * gram + third_coef * squared
    mixed = jnp.dot(poly, wide, precision=lax.Precision.HIGHEST)
    fresh = first_coef * wide + mixed
    return fresh.astype(jnp.bfloat16)


def on_device(grad, momentum, weight):
    mats, rows_local, cols_local = grad.shape
    n_tensor = lax.axis_size("tensor")
    new_momentum = mu_decay * momentum + grad
    advance = (grad + mu_decay * new_momentum).astype(jnp.bfloat16)
    mine = lax.all_to_all(advance, "tensor", split_axis=0, concat_axis=2, tiled=True)
    whole = lax.all_gather(mine, "shard", axis=1, tiled=True)[0]
    wide = whole.astype(jnp.float32)
    frob = jnp.sqrt(jnp.sum(wide * wide)) + epsilon
    iterate = (wide / frob).astype(jnp.bfloat16)
    for step in range(ITERS):
        gram = jnp.dot(iterate, iterate.T, preferred_element_type=jnp.float32)
        iterate = polish(iterate, gram)
    start = lax.axis_index("shard") * rows_local
    rows = lax.dynamic_slice_in_dim(iterate, start, rows_local, axis=0)
    ortho = lax.all_to_all(rows[None], "tensor", split_axis=2, concat_axis=0, tiled=True)
    width = cols_local * n_tensor
    update = update_gain * math.sqrt(width) * ortho.astype(jnp.float32)
    new_weight = weight - learn_rate * (update + weight_decay * weight)
    return (new_weight, new_momentum, update)


def solution(mesh):
    in_specs = (P(None, "shard", "tensor"), P(None, "shard", "tensor"), P(None, "shard", "tensor"))
    out_specs = (P(None, "shard", "tensor"), P(None, "shard", "tensor"), P(None, "shard", "tensor"))
    return jax.shard_map(
        on_device, mesh=mesh, in_specs=in_specs, out_specs=out_specs, check_vma=False
    )
```

```python
import math

import jax
import jax.numpy as jnp
from jax import lax
from jax.sharding import PartitionSpec as P

ITERS = 3
SHARD_AXES = ("sx", "sz", "sc")


mu_decay = 0.95
learn_rate = 0.05
weight_decay = 0.1
update_gain = 0.2
first_coef = 3.4445
second_coef = -4.775
third_coef = 2.0315
epsilon = 1e-07


def polish(iterate, gram):
    wide = iterate.astype(jnp.float32)
    squared = jnp.dot(gram, gram, precision=lax.Precision.HIGHEST)
    poly = second_coef * gram + third_coef * squared
    mixed = jnp.dot(poly, wide, precision=lax.Precision.HIGHEST)
    fresh = first_coef * wide + mixed
    return fresh.astype(jnp.bfloat16)


def on_device(grad, momentum, weight):
    mats, rows_local, cols_local = grad.shape
    n_tensor = lax.axis_size("tensor")
    new_momentum = mu_decay * momentum + grad
    advance = (grad + mu_decay * new_momentum).astype(jnp.bfloat16)
    mine = lax.all_to_all(advance, "tensor", split_axis=0, concat_axis=2, tiled=True)
    for axis in SHARD_AXES:
        mine = lax.all_gather(mine, axis, axis=1, tiled=True)
    whole = mine[0]
    wide = whole.astype(jnp.float32)
    frob = jnp.sqrt(jnp.sum(wide * wide)) + epsilon
    iterate = (wide / frob).astype(jnp.bfloat16)
    for step in range(ITERS):
        gram = jnp.dot(iterate, iterate.T, preferred_element_type=jnp.float32)
        iterate = polish(iterate, gram)
    block = 0
    for axis in reversed(SHARD_AXES):
        block = block * lax.axis_size(axis) + lax.axis_index(axis)
    start = block * rows_local
    rows = lax.dynamic_slice_in_dim(iterate, start, rows_local, axis=0)
    ortho = lax.all_to_all(rows[None], "tensor", split_axis=2, concat_axis=0, tiled=True)
    width = cols_local * n_tensor
    update = update_gain * math.sqrt(width) * ortho.astype(jnp.float32)
    new_weight = weight - learn_rate * (update + weight_decay * weight)
    return (new_weight, new_momentum, update)


def split_shard(mesh):
    devices = mesh.devices
    column = devices[:, 0]
    try:
        n_x = len({d.coords[0] for d in column})
        n_z = len({d.coords[2] for d in column})
        n_core = len({d.core_on_chip for d in column})
    except AttributeError:
        n_x, n_z, n_core = len(column), 1, 1
    if n_x * n_z * n_core != len(column):
        n_x, n_z, n_core = len(column), 1, 1
    grid = devices.reshape(n_x, n_z, n_core, devices.shape[1])
    return jax.sharding.Mesh(grid, SHARD_AXES + ("tensor",))


def solution(mesh):
    fine = split_shard(mesh)
    spec = P(None, SHARD_AXES, "tensor")
    return jax.shard_map(
        on_device, mesh=fine, in_specs=(spec,) * 3, out_specs=(spec,) * 3, check_vma=False
    )
```

```python
import math

import jax
import jax.numpy as jnp
from jax import lax
from jax.sharding import PartitionSpec as P

ITERS = 3
SHARD_AXES = ("sx", "sz", "sc")


mu_decay = 0.95
learn_rate = 0.05
weight_decay = 0.1
update_gain = 0.2
first_coef = 3.4445
second_coef = -4.775
third_coef = 2.0315
epsilon = 1e-07


def polish(iterate, gram):
    wide = iterate.astype(jnp.float32)
    squared = jnp.dot(gram, gram, precision=lax.Precision.HIGHEST)
    poly = second_coef * gram + third_coef * squared
    mixed = jnp.dot(poly, wide, precision=lax.Precision.HIGHEST)
    fresh = first_coef * wide + mixed
    return fresh.astype(jnp.bfloat16)


def on_device(grad, momentum, weight):
    mats, rows_local, cols_local = grad.shape
    n_tensor = lax.axis_size("tensor")
    new_momentum = mu_decay * momentum + grad
    advance = (grad + mu_decay * new_momentum).astype(jnp.bfloat16)
    n_shard = 1
    for axis in SHARD_AXES:
        n_shard *= lax.axis_size(axis)
    sent = jnp.broadcast_to(advance[None], (n_shard,) + advance.shape)
    sent = sent.reshape(n_shard * mats, rows_local, cols_local)
    got = lax.all_to_all(sent, SHARD_AXES + ("tensor",), split_axis=0, concat_axis=0, tiled=True)
    got = got.reshape(n_shard, n_tensor, rows_local, cols_local).transpose(0, 2, 1, 3)
    whole = got.reshape(n_shard * rows_local, n_tensor * cols_local)
    wide = whole.astype(jnp.float32)
    frob = jnp.sqrt(jnp.sum(wide * wide)) + epsilon
    iterate = (wide / frob).astype(jnp.bfloat16)
    for step in range(ITERS):
        gram = jnp.dot(iterate, iterate.T, preferred_element_type=jnp.float32)
        iterate = polish(iterate, gram)
    block = 0
    for axis in SHARD_AXES:
        block = block * lax.axis_size(axis) + lax.axis_index(axis)
    start = block * rows_local
    rows = lax.dynamic_slice_in_dim(iterate, start, rows_local, axis=0)
    ortho = lax.all_to_all(rows[None], "tensor", split_axis=2, concat_axis=0, tiled=True)
    width = cols_local * n_tensor
    update = update_gain * math.sqrt(width) * ortho.astype(jnp.float32)
    new_weight = weight - learn_rate * (update + weight_decay * weight)
    return (new_weight, new_momentum, update)


def split_shard(mesh):
    devices = mesh.devices
    column = devices[:, 0]
    try:
        n_x = len({d.coords[0] for d in column})
        n_z = len({d.coords[2] for d in column})
        n_core = len({d.core_on_chip for d in column})
    except AttributeError:
        n_x, n_z, n_core = len(column), 1, 1
    if n_x * n_z * n_core != len(column):
        n_x, n_z, n_core = len(column), 1, 1
    grid = devices.reshape(n_x, n_z, n_core, devices.shape[1])
    return jax.sharding.Mesh(grid, SHARD_AXES + ("tensor",))


def solution(mesh):
    fine = split_shard(mesh)
    spec = P(None, SHARD_AXES, "tensor")
    return jax.shard_map(
        on_device, mesh=fine, in_specs=(spec,) * 3, out_specs=(spec,) * 3, check_vma=False
    )
```

```python
import math

import jax
import jax.numpy as jnp
from jax import lax
from jax.sharding import PartitionSpec as P

ITERS = 3
SHARD_AXES = ("sx", "sz", "sc")


mu_decay = 0.95
learn_rate = 0.05
weight_decay = 0.1
update_gain = 0.2
first_coef = 3.4445
second_coef = -4.775
third_coef = 2.0315
epsilon = 1e-07


def split_dot(wide_lhs, rhs):
    high = wide_lhs.astype(jnp.bfloat16)
    low = (wide_lhs - high.astype(jnp.float32)).astype(jnp.bfloat16)
    both = jnp.concatenate([high, low], axis=1)
    return jnp.dot(both, jnp.concatenate([rhs, rhs], axis=0), preferred_element_type=jnp.float32)


def polish(iterate, gram, rows=None):
    squared_rows = gram if rows is None else rows(gram)
    squared = jnp.dot(squared_rows, gram, precision=lax.Precision.HIGH)
    poly = second_coef * squared_rows + third_coef * squared
    head = iterate if rows is None else rows(iterate)
    fresh = first_coef * head.astype(jnp.float32) + split_dot(poly, iterate)
    return fresh.astype(jnp.bfloat16)


def on_device(grad, momentum, weight):
    mats, rows_local, cols_local = grad.shape
    n_tensor = lax.axis_size("tensor")
    new_momentum = mu_decay * momentum + grad
    advance = (grad + mu_decay * new_momentum).astype(jnp.bfloat16)
    n_shard = 1
    for axis in SHARD_AXES:
        n_shard *= lax.axis_size(axis)
    sent = jnp.broadcast_to(advance[None], (n_shard,) + advance.shape)
    sent = sent.reshape(n_shard * mats, rows_local, cols_local)
    got = lax.all_to_all(sent, SHARD_AXES + ("tensor",), split_axis=0, concat_axis=0, tiled=True)
    got = got.reshape(n_shard, n_tensor, rows_local, cols_local).transpose(0, 2, 1, 3)
    whole = got.reshape(n_shard * rows_local, n_tensor * cols_local)
    wide = whole.astype(jnp.float32)
    frob = jnp.sqrt(jnp.sum(wide * wide)) + epsilon
    iterate = (wide / frob).astype(jnp.bfloat16)
    block = 0
    for axis in SHARD_AXES:
        block = block * lax.axis_size(axis) + lax.axis_index(axis)
    start = block * rows_local

    def mine(full):
        return lax.dynamic_slice_in_dim(full, start, rows_local, axis=0)

    for step in range(ITERS):
        gram = jnp.dot(iterate, iterate.T, preferred_element_type=jnp.float32)
        iterate = polish(iterate, gram, mine if step == ITERS - 1 else None)
    pieces = iterate.reshape(rows_local, n_tensor, cols_local).transpose(1, 0, 2)
    ortho = lax.all_to_all(pieces, "tensor", split_axis=0, concat_axis=0, tiled=True)
    width = cols_local * n_tensor
    update = update_gain * math.sqrt(width) * ortho.astype(jnp.float32)
    new_weight = weight - learn_rate * (update + weight_decay * weight)
    return (new_weight, new_momentum, update)


def split_shard(mesh):
    devices = mesh.devices
    column = devices[:, 0]
    try:
        n_x = len({d.coords[0] for d in column})
        n_z = len({d.coords[2] for d in column})
        n_core = len({d.core_on_chip for d in column})
    except AttributeError:
        n_x, n_z, n_core = len(column), 1, 1
    if n_x * n_z * n_core != len(column):
        n_x, n_z, n_core = len(column), 1, 1
    grid = devices.reshape(n_x, n_z, n_core, devices.shape[1])
    return jax.sharding.Mesh(grid, SHARD_AXES + ("tensor",))


def solution(mesh):
    fine = split_shard(mesh)
    spec = P(None, SHARD_AXES, "tensor")
    return jax.shard_map(
        on_device, mesh=fine, in_specs=(spec,) * 3, out_specs=(spec,) * 3, check_vma=False
    )
```

```python
import math

import jax
import jax.numpy as jnp
from jax import lax
from jax.experimental import pallas as pl
from jax.experimental.pallas import tpu as pltpu
from jax.sharding import PartitionSpec as P
import functools

ITERS = 3
SHARD_AXES = ("sx", "sz", "sc")


mu_decay = 0.95
learn_rate = 0.05
weight_decay = 0.1
update_gain = 0.2
first_coef = 3.4445
second_coef = -4.775
third_coef = 2.0315
epsilon = 1e-07


MESH = pl.DeviceIdType.MESH


def shard_coords(index, sizes):
    coords = []
    for size in reversed(sizes):
        coords.append(index % size)
        index = index // size
    return tuple(reversed(coords))


def gather_kernel(sizes, n_tensor, adv_ref, out_ref, row_buf, whole_buf,
                  send1, recv1, send2, recv2, local_sem):
    mats, rows, cols = adv_ref.shape
    n_shard = 1
    for size in sizes:
        n_shard *= size
    here = tuple(lax.axis_index(a) for a in SHARD_AXES)
    t = lax.axis_index("tensor")
    me = 0
    for axis, size in zip(SHARD_AXES, sizes):
        me = me * size + lax.axis_index(axis)

    def shard_peer(k):
        return shard_coords(lax.rem(me + k, n_shard), sizes)

    barrier = pltpu.get_barrier_semaphore()
    for k in range(1, n_tensor):
        pl.semaphore_signal(barrier, inc=1, device_id=here + (lax.rem(t + k, n_tensor),),
                            device_id_type=MESH)

    def greet(k, carry):
        pl.semaphore_signal(barrier, inc=1, device_id=shard_peer(k) + (t,), device_id_type=MESH)
        return carry

    lax.fori_loop(1, n_shard, greet, 0)
    pl.semaphore_wait(barrier, n_tensor - 1 + n_shard - 1)

    my_cols = pl.ds(pl.multiple_of(t * cols, cols), cols)
    own = pltpu.make_async_copy(adv_ref.at[t], row_buf.at[:, my_cols], local_sem)
    own.start()
    firsts = []
    for k in range(1, n_tensor):
        peer = lax.rem(t + k, n_tensor)
        copy = pltpu.make_async_remote_copy(
            src_ref=adv_ref.at[peer], dst_ref=row_buf.at[:, my_cols],
            send_sem=send1.at[peer], recv_sem=recv1.at[t],
            device_id=here + (peer,), device_id_type=MESH)
        copy.start()
        firsts.append(copy)
    own.wait()
    for k in range(1, n_tensor):
        peer = lax.rem(t + k, n_tensor)
        peer_cols = pl.ds(pl.multiple_of(peer * cols, cols), cols)
        pltpu.make_async_remote_copy(
            src_ref=adv_ref.at[t], dst_ref=row_buf.at[:, peer_cols],
            send_sem=send1.at[peer], recv_sem=recv1.at[peer],
            device_id=here + (peer,), device_id_type=MESH).wait_recv()
        firsts[k - 1].wait_send()

    my_rows = pl.ds(pl.multiple_of(me * rows, rows), rows)
    own = pltpu.make_async_copy(row_buf, whole_buf.at[my_rows], local_sem)
    own.start()

    def send(k, carry):
        peer = lax.rem(me + k, n_shard)
        pltpu.make_async_remote_copy(
            src_ref=row_buf, dst_ref=whole_buf.at[my_rows],
            send_sem=send2.at[peer], recv_sem=recv2.at[me],
            device_id=shard_coords(peer, sizes) + (t,), device_id_type=MESH).start()
        return carry

    lax.fori_loop(1, n_shard, send, 0)
    own.wait()

    def finish(k, carry):
        peer = lax.rem(me + k, n_shard)
        peer_rows = pl.ds(pl.multiple_of(peer * rows, rows), rows)
        copy = pltpu.make_async_remote_copy(
            src_ref=row_buf, dst_ref=whole_buf.at[peer_rows],
            send_sem=send2.at[peer], recv_sem=recv2.at[peer],
            device_id=shard_coords(peer, sizes) + (t,), device_id_type=MESH)
        copy.wait_recv()
        copy.wait_send()
        return carry

    lax.fori_loop(1, n_shard, finish, 0)
    out_ref[...] = whole_buf[...]


def gather(advance, sizes, n_tensor):
    mats, rows, cols = advance.shape
    n_shard = 1
    for size in sizes:
        n_shard *= size
    return pl.pallas_call(
        functools.partial(gather_kernel, sizes, n_tensor),
        out_shape=jax.ShapeDtypeStruct((n_shard * rows, n_tensor * cols), advance.dtype),
        in_specs=[pl.BlockSpec(memory_space=pltpu.VMEM)],
        out_specs=pl.BlockSpec(memory_space=pltpu.VMEM),
        scratch_shapes=[
            pltpu.VMEM((rows, n_tensor * cols), advance.dtype),
            pltpu.VMEM((n_shard * rows, n_tensor * cols), advance.dtype),
            pltpu.SemaphoreType.DMA((n_tensor,)),
            pltpu.SemaphoreType.DMA((n_tensor,)),
            pltpu.SemaphoreType.DMA((n_shard,)),
            pltpu.SemaphoreType.DMA((n_shard,)),
            pltpu.SemaphoreType.DMA,
        ],
        compiler_params=pltpu.CompilerParams(collective_id=0, has_side_effects=True),
    )(advance)


def split_dot(wide_lhs, rhs):
    high = wide_lhs.astype(jnp.bfloat16)
    low = (wide_lhs - high.astype(jnp.float32)).astype(jnp.bfloat16)
    both = jnp.concatenate([high, low], axis=1)
    return jnp.dot(both, jnp.concatenate([rhs, rhs], axis=0), preferred_element_type=jnp.float32)


def polish(iterate, gram, rows=None):
    squared_rows = gram if rows is None else rows(gram)
    squared = jnp.dot(squared_rows, gram, precision=lax.Precision.HIGH)
    poly = second_coef * squared_rows + third_coef * squared
    head = iterate if rows is None else rows(iterate)
    fresh = first_coef * head.astype(jnp.float32) + split_dot(poly, iterate)
    return fresh.astype(jnp.bfloat16)


def on_device(grad, momentum, weight):
    mats, rows_local, cols_local = grad.shape
    n_tensor = lax.axis_size("tensor")
    new_momentum = mu_decay * momentum + grad
    advance = (grad + mu_decay * new_momentum).astype(jnp.bfloat16)
    sizes = tuple(lax.axis_size(axis) for axis in SHARD_AXES)
    whole = gather(advance, sizes, n_tensor)
    wide = whole.astype(jnp.float32)
    frob = jnp.sqrt(jnp.sum(wide * wide)) + epsilon
    iterate = (wide / frob).astype(jnp.bfloat16)
    block = 0
    for axis in SHARD_AXES:
        block = block * lax.axis_size(axis) + lax.axis_index(axis)
    start = block * rows_local

    def mine(full):
        return lax.dynamic_slice_in_dim(full, start, rows_local, axis=0)

    for step in range(ITERS):
        gram = jnp.dot(iterate, iterate.T, preferred_element_type=jnp.float32)
        iterate = polish(iterate, gram, mine if step == ITERS - 1 else None)
    pieces = iterate.reshape(rows_local, n_tensor, cols_local).transpose(1, 0, 2)
    ortho = lax.all_to_all(pieces, "tensor", split_axis=0, concat_axis=0, tiled=True)
    width = cols_local * n_tensor
    update = update_gain * math.sqrt(width) * ortho.astype(jnp.float32)
    new_weight = weight - learn_rate * (update + weight_decay * weight)
    return (new_weight, new_momentum, update)


def split_shard(mesh):
    devices = mesh.devices
    column = devices[:, 0]
    try:
        n_x = len({d.coords[0] for d in column})
        n_z = len({d.coords[2] for d in column})
        n_core = len({d.core_on_chip for d in column})
    except AttributeError:
        n_x, n_z, n_core = len(column), 1, 1
    if n_x * n_z * n_core != len(column):
        n_x, n_z, n_core = len(column), 1, 1
    grid = devices.reshape(n_x, n_z, n_core, devices.shape[1])
    return jax.sharding.Mesh(grid, SHARD_AXES + ("tensor",))


def solution(mesh):
    fine = split_shard(mesh)
    spec = P(None, SHARD_AXES, "tensor")
    return jax.shard_map(
        on_device, mesh=fine, in_specs=(spec,) * 3, out_specs=(spec,) * 3, check_vma=False
    )
```

```python
import math

import jax
import jax.numpy as jnp
from jax import lax
from jax.experimental import pallas as pl
from jax.experimental.pallas import tpu as pltpu
from jax.sharding import PartitionSpec as P
import functools

ITERS = 3
SHARD_AXES = ("sx", "sz", "sc")


mu_decay = 0.95
learn_rate = 0.05
weight_decay = 0.1
update_gain = 0.2
first_coef = 3.4445
second_coef = -4.775
third_coef = 2.0315
epsilon = 1e-07


MESH = pl.DeviceIdType.MESH


def shard_coords(index, sizes):
    coords = []
    for size in reversed(sizes):
        coords.append(index % size)
        index = index // size
    return tuple(reversed(coords))


def gather_kernel(sizes, n_tensor, adv_ref, out_ref, row_buf, whole_buf,
                  send1, recv1, send2, recv2, local_sem):
    mats, rows, cols = adv_ref.shape
    n_shard = 1
    for size in sizes:
        n_shard *= size
    here = tuple(lax.axis_index(a) for a in SHARD_AXES)
    t = lax.axis_index("tensor")
    me = 0
    for axis, size in zip(SHARD_AXES, sizes):
        me = me * size + lax.axis_index(axis)

    def shard_peer(k):
        return shard_coords(lax.rem(me + k, n_shard), sizes)

    barrier = pltpu.get_barrier_semaphore()
    for k in range(1, n_tensor):
        pl.semaphore_signal(barrier, inc=1, device_id=here + (lax.rem(t + k, n_tensor),),
                            device_id_type=MESH)

    def greet(k, carry):
        pl.semaphore_signal(barrier, inc=1, device_id=shard_peer(k) + (t,), device_id_type=MESH)
        return carry

    lax.fori_loop(1, n_shard, greet, 0)
    pl.semaphore_wait(barrier, n_tensor - 1 + n_shard - 1)

    my_cols = pl.ds(pl.multiple_of(t * cols, cols), cols)
    own = pltpu.make_async_copy(adv_ref.at[t], row_buf.at[:, my_cols], local_sem)
    own.start()
    firsts = []
    for k in range(1, n_tensor):
        peer = lax.rem(t + k, n_tensor)
        copy = pltpu.make_async_remote_copy(
            src_ref=adv_ref.at[peer], dst_ref=row_buf.at[:, my_cols],
            send_sem=send1.at[peer], recv_sem=recv1.at[t],
            device_id=here + (peer,), device_id_type=MESH)
        copy.start()
        firsts.append(copy)
    own.wait()
    for k in range(1, n_tensor):
        peer = lax.rem(t + k, n_tensor)
        peer_cols = pl.ds(pl.multiple_of(peer * cols, cols), cols)
        pltpu.make_async_remote_copy(
            src_ref=adv_ref.at[t], dst_ref=row_buf.at[:, peer_cols],
            send_sem=send1.at[peer], recv_sem=recv1.at[peer],
            device_id=here + (peer,), device_id_type=MESH).wait_recv()
        firsts[k - 1].wait_send()

    my_rows = pl.ds(pl.multiple_of(me * rows, rows), rows)
    own = pltpu.make_async_copy(row_buf, whole_buf.at[my_rows], local_sem)
    own.start()

    def send(k, carry):
        peer = lax.rem(me + k, n_shard)
        pltpu.make_async_remote_copy(
            src_ref=row_buf, dst_ref=whole_buf.at[my_rows],
            send_sem=send2.at[peer], recv_sem=recv2.at[me],
            device_id=shard_coords(peer, sizes) + (t,), device_id_type=MESH).start()
        return carry

    lax.fori_loop(1, n_shard, send, 0)
    own.wait()

    def finish(k, carry):
        peer = lax.rem(me + k, n_shard)
        peer_rows = pl.ds(pl.multiple_of(peer * rows, rows), rows)
        copy = pltpu.make_async_remote_copy(
            src_ref=row_buf, dst_ref=whole_buf.at[peer_rows],
            send_sem=send2.at[peer], recv_sem=recv2.at[peer],
            device_id=shard_coords(peer, sizes) + (t,), device_id_type=MESH)
        copy.wait_recv()
        copy.wait_send()
        return carry

    lax.fori_loop(1, n_shard, finish, 0)
    out_ref[...] = whole_buf[...]


def gather(advance, sizes, n_tensor):
    mats, rows, cols = advance.shape
    n_shard = 1
    for size in sizes:
        n_shard *= size
    return pl.pallas_call(
        functools.partial(gather_kernel, sizes, n_tensor),
        out_shape=jax.ShapeDtypeStruct((n_shard * rows, n_tensor * cols), advance.dtype),
        in_specs=[pl.BlockSpec(memory_space=pltpu.VMEM)],
        out_specs=pl.BlockSpec(memory_space=pltpu.VMEM),
        scratch_shapes=[
            pltpu.VMEM((rows, n_tensor * cols), advance.dtype),
            pltpu.VMEM((n_shard * rows, n_tensor * cols), advance.dtype),
            pltpu.SemaphoreType.DMA((n_tensor,)),
            pltpu.SemaphoreType.DMA((n_tensor,)),
            pltpu.SemaphoreType.DMA((n_shard,)),
            pltpu.SemaphoreType.DMA((n_shard,)),
            pltpu.SemaphoreType.DMA,
        ],
        compiler_params=pltpu.CompilerParams(collective_id=0, has_side_effects=True),
    )(advance)


def gather2_kernel(sizes, n_tensor, adv_ref, out_ref, row_buf, whole_buf,
                   send1, recv1, send2, recv2, fwd, local_sem):
    mats, rows, cols = adv_ref.shape
    n_core = sizes[-1]
    n_chip = 1
    for size in sizes[:-1]:
        n_chip *= size
    n_shard = n_chip * n_core
    here = tuple(lax.axis_index(a) for a in SHARD_AXES)
    t = lax.axis_index("tensor")
    me = 0
    for axis, size in zip(SHARD_AXES, sizes):
        me = me * size + lax.axis_index(axis)
    core = lax.rem(me, n_core)
    chip = me // n_core

    def device(index):
        return shard_coords(index, sizes) + (t,)

    def chip_peer(k):
        return lax.rem(chip + k, n_chip) * n_core + core

    def sibling(j):
        return chip * n_core + lax.rem(core + j, n_core)

    barrier = pltpu.get_barrier_semaphore()
    for k in range(1, n_tensor):
        pl.semaphore_signal(barrier, inc=1, device_id=here + (lax.rem(t + k, n_tensor),),
                            device_id_type=MESH)

    def greet(k, carry):
        pl.semaphore_signal(barrier, inc=1, device_id=device(chip_peer(k)), device_id_type=MESH)
        return carry

    lax.fori_loop(1, n_chip, greet, 0)
    for j in range(1, n_core):
        pl.semaphore_signal(barrier, inc=1, device_id=device(sibling(j)), device_id_type=MESH)
    pl.semaphore_wait(barrier, n_tensor - 1 + n_chip - 1 + n_core - 1)

    my_cols = pl.ds(pl.multiple_of(t * cols, cols), cols)
    own = pltpu.make_async_copy(adv_ref.at[t], row_buf.at[:, my_cols], local_sem)
    own.start()
    firsts = []
    for k in range(1, n_tensor):
        peer = lax.rem(t + k, n_tensor)
        copy = pltpu.make_async_remote_copy(
            src_ref=adv_ref.at[peer], dst_ref=row_buf.at[:, my_cols],
            send_sem=send1.at[peer], recv_sem=recv1.at[t],
            device_id=here + (peer,), device_id_type=MESH)
        copy.start()
        firsts.append(copy)
    own.wait()
    for k in range(1, n_tensor):
        peer = lax.rem(t + k, n_tensor)
        peer_cols = pl.ds(pl.multiple_of(peer * cols, cols), cols)
        pltpu.make_async_remote_copy(
            src_ref=adv_ref.at[t], dst_ref=row_buf.at[:, peer_cols],
            send_sem=send1.at[peer], recv_sem=recv1.at[peer],
            device_id=here + (peer,), device_id_type=MESH).wait_recv()
        firsts[k - 1].wait_send()

    def rows_of(index):
        return pl.ds(pl.multiple_of(index * rows, rows), rows)

    def direct(dest):
        return pltpu.make_async_remote_copy(
            src_ref=row_buf, dst_ref=whole_buf.at[rows_of(me)],
            send_sem=send2.at[dest], recv_sem=recv2.at[me],
            device_id=device(dest), device_id_type=MESH)

    def send(k, carry):
        direct(chip_peer(k)).start()
        return carry

    lax.fori_loop(1, n_chip, send, 0)
    for j in range(1, n_core):
        direct(sibling(j)).start()
    own = pltpu.make_async_copy(row_buf, whole_buf.at[rows_of(me)], local_sem)
    own.start()

    def forward(source, dest):
        return pltpu.make_async_remote_copy(
            src_ref=whole_buf.at[rows_of(source)], dst_ref=whole_buf.at[rows_of(source)],
            send_sem=fwd.at[source], recv_sem=recv2.at[source],
            device_id=device(dest), device_id_type=MESH)

    def relay(k, carry):
        source = chip_peer(k)
        pltpu.make_async_remote_copy(
            src_ref=row_buf, dst_ref=whole_buf.at[rows_of(source)],
            send_sem=send2.at[source], recv_sem=recv2.at[source],
            device_id=device(source), device_id_type=MESH).wait_recv()
        for j in range(1, n_core):
            forward(source, sibling(j)).start()
        return carry

    lax.fori_loop(1, n_chip, relay, 0)
    own.wait()

    def settle(k, carry):
        source = chip_peer(k)
        direct(source).wait_send()
        for j in range(1, n_core):
            forward(source, sibling(j)).wait_send()
            other = source - core + lax.rem(core + j, n_core)
            forward(other, sibling(j)).wait_recv()
        return carry

    lax.fori_loop(1, n_chip, settle, 0)
    for j in range(1, n_core):
        direct(sibling(j)).wait_send()
        pltpu.make_async_remote_copy(
            src_ref=row_buf, dst_ref=whole_buf.at[rows_of(sibling(j))],
            send_sem=send2.at[sibling(j)], recv_sem=recv2.at[sibling(j)],
            device_id=device(sibling(j)), device_id_type=MESH).wait_recv()
    out_ref[...] = whole_buf[...]


def gather2(advance, sizes, n_tensor):
    mats, rows, cols = advance.shape
    n_shard = 1
    for size in sizes:
        n_shard *= size
    return pl.pallas_call(
        functools.partial(gather2_kernel, sizes, n_tensor),
        out_shape=jax.ShapeDtypeStruct((n_shard * rows, n_tensor * cols), advance.dtype),
        in_specs=[pl.BlockSpec(memory_space=pltpu.VMEM)],
        out_specs=pl.BlockSpec(memory_space=pltpu.VMEM),
        scratch_shapes=[
            pltpu.VMEM((rows, n_tensor * cols), advance.dtype),
            pltpu.VMEM((n_shard * rows, n_tensor * cols), advance.dtype),
            pltpu.SemaphoreType.DMA((n_tensor,)),
            pltpu.SemaphoreType.DMA((n_tensor,)),
            pltpu.SemaphoreType.DMA((n_shard,)),
            pltpu.SemaphoreType.DMA((n_shard,)),
            pltpu.SemaphoreType.DMA((n_shard,)),
            pltpu.SemaphoreType.DMA,
        ],
        compiler_params=pltpu.CompilerParams(collective_id=0, has_side_effects=True),
    )(advance)


def split_dot(wide_lhs, rhs):
    high = wide_lhs.astype(jnp.bfloat16)
    low = (wide_lhs - high.astype(jnp.float32)).astype(jnp.bfloat16)
    both = jnp.concatenate([high, low], axis=1)
    return jnp.dot(both, jnp.concatenate([rhs, rhs], axis=0), preferred_element_type=jnp.float32)


def polish(iterate, gram, rows=None):
    squared_rows = gram if rows is None else rows(gram)
    squared = jnp.dot(squared_rows, gram, precision=lax.Precision.HIGH)
    poly = second_coef * squared_rows + third_coef * squared
    head = iterate if rows is None else rows(iterate)
    fresh = first_coef * head.astype(jnp.float32) + split_dot(poly, iterate)
    return fresh.astype(jnp.bfloat16)


def on_device(grad, momentum, weight):
    mats, rows_local, cols_local = grad.shape
    n_tensor = lax.axis_size("tensor")
    new_momentum = mu_decay * momentum + grad
    advance = (grad + mu_decay * new_momentum).astype(jnp.bfloat16)
    sizes = tuple(lax.axis_size(axis) for axis in SHARD_AXES)
    whole = gather2(advance, sizes, n_tensor)
    wide = whole.astype(jnp.float32)
    frob = jnp.sqrt(jnp.sum(wide * wide)) + epsilon
    iterate = (wide / frob).astype(jnp.bfloat16)
    block = 0
    for axis in SHARD_AXES:
        block = block * lax.axis_size(axis) + lax.axis_index(axis)
    start = block * rows_local

    def mine(full):
        return lax.dynamic_slice_in_dim(full, start, rows_local, axis=0)

    for step in range(ITERS):
        gram = jnp.dot(iterate, iterate.T, preferred_element_type=jnp.float32)
        iterate = polish(iterate, gram, mine if step == ITERS - 1 else None)
    pieces = iterate.reshape(rows_local, n_tensor, cols_local).transpose(1, 0, 2)
    ortho = lax.all_to_all(pieces, "tensor", split_axis=0, concat_axis=0, tiled=True)
    width = cols_local * n_tensor
    update = update_gain * math.sqrt(width) * ortho.astype(jnp.float32)
    new_weight = weight - learn_rate * (update + weight_decay * weight)
    return (new_weight, new_momentum, update)


def split_shard(mesh):
    devices = mesh.devices
    column = devices[:, 0]
    try:
        n_x = len({d.coords[0] for d in column})
        n_z = len({d.coords[2] for d in column})
        n_core = len({d.core_on_chip for d in column})
    except AttributeError:
        n_x, n_z, n_core = len(column), 1, 1
    if n_x * n_z * n_core != len(column):
        n_x, n_z, n_core = len(column), 1, 1
    grid = devices.reshape(n_x, n_z, n_core, devices.shape[1])
    return jax.sharding.Mesh(grid, SHARD_AXES + ("tensor",))


def solution(mesh):
    fine = split_shard(mesh)
    spec = P(None, SHARD_AXES, "tensor")
    return jax.shard_map(
        on_device, mesh=fine, in_specs=(spec,) * 3, out_specs=(spec,) * 3, check_vma=False
    )
```

```python
import math

import jax
import jax.numpy as jnp
from jax import lax
from jax.experimental import pallas as pl
from jax.experimental.pallas import tpu as pltpu
from jax.sharding import PartitionSpec as P
import functools

ITERS = 3
SHARD_AXES = ("sx", "sz", "sc")


mu_decay = 0.95
learn_rate = 0.05
weight_decay = 0.1
update_gain = 0.2
first_coef = 3.4445
second_coef = -4.775
third_coef = 2.0315
epsilon = 1e-07


MESH = pl.DeviceIdType.MESH


def shard_coords(index, sizes):
    coords = []
    for size in reversed(sizes):
        coords.append(index % size)
        index = index // size
    return tuple(reversed(coords))


def gather2_kernel(sizes, n_tensor, adv_ref, out_ref, row_buf, whole_buf,
                   send1, recv1, send2, recv2, fwd, local_sem):
    mats, rows, cols = adv_ref.shape
    n_core = sizes[-1]
    n_chip = 1
    for size in sizes[:-1]:
        n_chip *= size
    n_shard = n_chip * n_core
    here = tuple(lax.axis_index(a) for a in SHARD_AXES)
    t = lax.axis_index("tensor")
    me = 0
    for axis, size in zip(SHARD_AXES, sizes):
        me = me * size + lax.axis_index(axis)
    core = lax.rem(me, n_core)
    chip = me // n_core

    def device(index):
        return shard_coords(index, sizes) + (t,)

    def chip_peer(k):
        return lax.rem(chip + k, n_chip) * n_core + core

    def sibling(j):
        return chip * n_core + lax.rem(core + j, n_core)

    barrier = pltpu.get_barrier_semaphore()
    for k in range(1, n_tensor):
        pl.semaphore_signal(barrier, inc=1, device_id=here + (lax.rem(t + k, n_tensor),),
                            device_id_type=MESH)

    def greet(k, carry):
        pl.semaphore_signal(barrier, inc=1, device_id=device(chip_peer(k)), device_id_type=MESH)
        return carry

    lax.fori_loop(1, n_chip, greet, 0)
    for j in range(1, n_core):
        pl.semaphore_signal(barrier, inc=1, device_id=device(sibling(j)), device_id_type=MESH)
    pl.semaphore_wait(barrier, n_tensor - 1 + n_chip - 1 + n_core - 1)

    my_cols = pl.ds(pl.multiple_of(t * cols, cols), cols)
    own = pltpu.make_async_copy(adv_ref.at[t], row_buf.at[:, my_cols], local_sem)
    own.start()
    firsts = []
    for k in range(1, n_tensor):
        peer = lax.rem(t + k, n_tensor)
        copy = pltpu.make_async_remote_copy(
            src_ref=adv_ref.at[peer], dst_ref=row_buf.at[:, my_cols],
            send_sem=send1.at[peer], recv_sem=recv1.at[t],
            device_id=here + (peer,), device_id_type=MESH)
        copy.start()
        firsts.append(copy)
    own.wait()
    for k in range(1, n_tensor):
        peer = lax.rem(t + k, n_tensor)
        peer_cols = pl.ds(pl.multiple_of(peer * cols, cols), cols)
        pltpu.make_async_remote_copy(
            src_ref=adv_ref.at[t], dst_ref=row_buf.at[:, peer_cols],
            send_sem=send1.at[peer], recv_sem=recv1.at[peer],
            device_id=here + (peer,), device_id_type=MESH).wait_recv()
        firsts[k - 1].wait_send()

    def rows_of(index):
        return pl.ds(pl.multiple_of(index * rows, rows), rows)

    def direct(dest):
        return pltpu.make_async_remote_copy(
            src_ref=row_buf, dst_ref=whole_buf.at[rows_of(me)],
            send_sem=send2.at[dest], recv_sem=recv2.at[me],
            device_id=device(dest), device_id_type=MESH)

    def send(k, carry):
        direct(chip_peer(k)).start()
        return carry

    lax.fori_loop(1, n_chip, send, 0)
    for j in range(1, n_core):
        direct(sibling(j)).start()
    own = pltpu.make_async_copy(row_buf, whole_buf.at[rows_of(me)], local_sem)
    own.start()

    def forward(source, dest):
        return pltpu.make_async_remote_copy(
            src_ref=whole_buf.at[rows_of(source)], dst_ref=whole_buf.at[rows_of(source)],
            send_sem=fwd.at[source], recv_sem=recv2.at[source],
            device_id=device(dest), device_id_type=MESH)

    def relay(k, carry):
        source = chip_peer(k)
        pltpu.make_async_remote_copy(
            src_ref=row_buf, dst_ref=whole_buf.at[rows_of(source)],
            send_sem=send2.at[source], recv_sem=recv2.at[source],
            device_id=device(source), device_id_type=MESH).wait_recv()
        for j in range(1, n_core):
            forward(source, sibling(j)).start()
        return carry

    lax.fori_loop(1, n_chip, relay, 0)
    own.wait()

    def settle(k, carry):
        source = chip_peer(k)
        direct(source).wait_send()
        for j in range(1, n_core):
            forward(source, sibling(j)).wait_send()
            other = source - core + lax.rem(core + j, n_core)
            forward(other, sibling(j)).wait_recv()
        return carry

    lax.fori_loop(1, n_chip, settle, 0)
    for j in range(1, n_core):
        direct(sibling(j)).wait_send()
        pltpu.make_async_remote_copy(
            src_ref=row_buf, dst_ref=whole_buf.at[rows_of(sibling(j))],
            send_sem=send2.at[sibling(j)], recv_sem=recv2.at[sibling(j)],
            device_id=device(sibling(j)), device_id_type=MESH).wait_recv()
    out_ref[...] = whole_buf[...]


def gather2(advance, sizes, n_tensor):
    mats, rows, cols = advance.shape
    n_shard = 1
    for size in sizes:
        n_shard *= size
    return pl.pallas_call(
        functools.partial(gather2_kernel, sizes, n_tensor),
        out_shape=jax.ShapeDtypeStruct((n_shard * rows, n_tensor * cols), advance.dtype),
        in_specs=[pl.BlockSpec(memory_space=pltpu.VMEM)],
        out_specs=pl.BlockSpec(memory_space=pltpu.VMEM),
        scratch_shapes=[
            pltpu.VMEM((rows, n_tensor * cols), advance.dtype),
            pltpu.VMEM((n_shard * rows, n_tensor * cols), advance.dtype),
            pltpu.SemaphoreType.DMA((n_tensor,)),
            pltpu.SemaphoreType.DMA((n_tensor,)),
            pltpu.SemaphoreType.DMA((n_shard,)),
            pltpu.SemaphoreType.DMA((n_shard,)),
            pltpu.SemaphoreType.DMA((n_shard,)),
            pltpu.SemaphoreType.DMA,
        ],
        compiler_params=pltpu.CompilerParams(collective_id=0, has_side_effects=True),
    )(advance)


def scatter_kernel(n_tensor, piece_ref, out_ref, out_buf, send_sem, recv_sem, local_sem):
    here = tuple(lax.axis_index(a) for a in SHARD_AXES)
    t = lax.axis_index("tensor")
    barrier = pltpu.get_barrier_semaphore()
    for k in range(1, n_tensor):
        pl.semaphore_signal(barrier, inc=1, device_id=here + (lax.rem(t + k, n_tensor),),
                            device_id_type=MESH)
    pl.semaphore_wait(barrier, n_tensor - 1)
    own = pltpu.make_async_copy(piece_ref.at[t], out_buf.at[t], local_sem)
    own.start()
    copies = []
    for k in range(1, n_tensor):
        peer = lax.rem(t + k, n_tensor)
        copy = pltpu.make_async_remote_copy(
            src_ref=piece_ref.at[peer], dst_ref=out_buf.at[t],
            send_sem=send_sem.at[peer], recv_sem=recv_sem.at[t],
            device_id=here + (peer,), device_id_type=MESH)
        copy.start()
        copies.append(copy)
    own.wait()
    for k in range(1, n_tensor):
        peer = lax.rem(t + k, n_tensor)
        pltpu.make_async_remote_copy(
            src_ref=piece_ref.at[t], dst_ref=out_buf.at[peer],
            send_sem=send_sem.at[peer], recv_sem=recv_sem.at[peer],
            device_id=here + (peer,), device_id_type=MESH).wait_recv()
        copies[k - 1].wait_send()
    out_ref[...] = out_buf[...]


def scatter(pieces):
    n_tensor = pieces.shape[0]
    return pl.pallas_call(
        functools.partial(scatter_kernel, n_tensor),
        out_shape=jax.ShapeDtypeStruct(pieces.shape, pieces.dtype),
        in_specs=[pl.BlockSpec(memory_space=pltpu.VMEM)],
        out_specs=pl.BlockSpec(memory_space=pltpu.VMEM),
        scratch_shapes=[
            pltpu.VMEM(pieces.shape, pieces.dtype),
            pltpu.SemaphoreType.DMA((n_tensor,)),
            pltpu.SemaphoreType.DMA((n_tensor,)),
            pltpu.SemaphoreType.DMA,
        ],
        compiler_params=pltpu.CompilerParams(collective_id=1, has_side_effects=True),
    )(pieces)


def split_dot(wide_lhs, rhs):
    high = wide_lhs.astype(jnp.bfloat16)
    low = (wide_lhs - high.astype(jnp.float32)).astype(jnp.bfloat16)
    both = jnp.concatenate([high, low], axis=1)
    return jnp.dot(both, jnp.concatenate([rhs, rhs], axis=0), preferred_element_type=jnp.float32)


def polish(iterate, gram, rows=None):
    squared_rows = gram if rows is None else rows(gram)
    squared = jnp.dot(squared_rows, gram, precision=lax.Precision.HIGH)
    poly = second_coef * squared_rows + third_coef * squared
    head = iterate if rows is None else rows(iterate)
    fresh = first_coef * head.astype(jnp.float32) + split_dot(poly, iterate)
    return fresh.astype(jnp.bfloat16)


def on_device(grad, momentum, weight):
    mats, rows_local, cols_local = grad.shape
    n_tensor = lax.axis_size("tensor")
    new_momentum = mu_decay * momentum + grad
    advance = (grad + mu_decay * new_momentum).astype(jnp.bfloat16)
    sizes = tuple(lax.axis_size(axis) for axis in SHARD_AXES)
    whole = gather2(advance, sizes, n_tensor)
    wide = whole.astype(jnp.float32)
    frob = jnp.sqrt(jnp.sum(wide * wide)) + epsilon
    iterate = (wide / frob).astype(jnp.bfloat16)
    block = 0
    for axis in SHARD_AXES:
        block = block * lax.axis_size(axis) + lax.axis_index(axis)
    start = block * rows_local

    def mine(full):
        return lax.dynamic_slice_in_dim(full, start, rows_local, axis=0)

    for step in range(ITERS):
        gram = jnp.dot(iterate, iterate.T, preferred_element_type=jnp.float32)
        iterate = polish(iterate, gram, mine if step == ITERS - 1 else None)
    pieces = iterate.reshape(rows_local, n_tensor, cols_local).transpose(1, 0, 2)
    ortho = scatter(pieces)
    width = cols_local * n_tensor
    update = update_gain * math.sqrt(width) * ortho.astype(jnp.float32)
    new_weight = weight - learn_rate * (update + weight_decay * weight)
    return (new_weight, new_momentum, update)


def split_shard(mesh):
    devices = mesh.devices
    column = devices[:, 0]
    try:
        n_x = len({d.coords[0] for d in column})
        n_z = len({d.coords[2] for d in column})
        n_core = len({d.core_on_chip for d in column})
    except AttributeError:
        n_x, n_z, n_core = len(column), 1, 1
    if n_x * n_z * n_core != len(column):
        n_x, n_z, n_core = len(column), 1, 1
    grid = devices.reshape(n_x, n_z, n_core, devices.shape[1])
    return jax.sharding.Mesh(grid, SHARD_AXES + ("tensor",))


def solution(mesh):
    fine = split_shard(mesh)
    spec = P(None, SHARD_AXES, "tensor")
    return jax.shard_map(
        on_device, mesh=fine, in_specs=(spec,) * 3, out_specs=(spec,) * 3, check_vma=False
    )
```

```python
import math

import jax
import jax.numpy as jnp
from jax import lax
from jax.experimental import pallas as pl
from jax.experimental.pallas import tpu as pltpu
from jax.sharding import PartitionSpec as P
import functools

ITERS = 3
SHARD_AXES = ("sx", "sz", "sc")


mu_decay = 0.95
learn_rate = 0.05
weight_decay = 0.1
update_gain = 0.2
first_coef = 3.4445
second_coef = -4.775
third_coef = 2.0315
epsilon = 1e-07


MESH = pl.DeviceIdType.MESH


def shard_coords(index, sizes):
    coords = []
    for size in reversed(sizes):
        coords.append(index % size)
        index = index // size
    return tuple(reversed(coords))


def gather3_kernel(sizes, n_tensor, adv_ref, out_ref, row_buf, whole_buf,
                   send1, recv1, send_x, recv_x, send_z, recv_z, send_c, recv_c, local_sem):
    mats, rows, cols = adv_ref.shape
    n_x, n_z, n_c = sizes
    x, z, c = (lax.axis_index(a) for a in SHARD_AXES)
    here = (x, z, c)
    t = lax.axis_index("tensor")

    def block(bx, bz, bc):
        return (bc * n_z + bz) * n_x + bx

    def span(first, count):
        return pl.ds(pl.multiple_of(first * rows, rows), count * rows)

    barrier = pltpu.get_barrier_semaphore()
    peers = [here + (lax.rem(t + k, n_tensor),) for k in range(1, n_tensor)]
    peers += [(lax.rem(x + k, n_x), z, c, t) for k in range(1, n_x)]
    peers += [(x, lax.rem(z + k, n_z), c, t) for k in range(1, n_z)]
    peers += [(x, z, lax.rem(c + k, n_c), t) for k in range(1, n_c)]
    for peer in peers:
        pl.semaphore_signal(barrier, inc=1, device_id=peer, device_id_type=MESH)
    pl.semaphore_wait(barrier, len(peers))

    my_cols = pl.ds(pl.multiple_of(t * cols, cols), cols)
    own = pltpu.make_async_copy(adv_ref.at[t], row_buf.at[:, my_cols], local_sem)
    own.start()
    sent = []
    for k in range(1, n_tensor):
        peer = lax.rem(t + k, n_tensor)
        copy = pltpu.make_async_remote_copy(
            src_ref=adv_ref.at[peer], dst_ref=row_buf.at[:, my_cols],
            send_sem=send1.at[peer], recv_sem=recv1.at[t],
            device_id=here + (peer,), device_id_type=MESH)
        copy.start()
        sent.append(copy)
    own.wait()
    for k in range(1, n_tensor):
        peer = lax.rem(t + k, n_tensor)
        peer_cols = pl.ds(pl.multiple_of(peer * cols, cols), cols)
        pltpu.make_async_remote_copy(
            src_ref=adv_ref.at[t], dst_ref=row_buf.at[:, peer_cols],
            send_sem=send1.at[peer], recv_sem=recv1.at[peer],
            device_id=here + (peer,), device_id_type=MESH).wait_recv()
    for copy in sent:
        copy.wait_send()

    mine = span(block(x, z, c), 1)
    own = pltpu.make_async_copy(row_buf, whole_buf.at[mine], local_sem)
    own.start()
    sent = []
    for k in range(1, n_x):
        peer = lax.rem(x + k, n_x)
        copy = pltpu.make_async_remote_copy(
            src_ref=row_buf, dst_ref=whole_buf.at[mine],
            send_sem=send_x.at[peer], recv_sem=recv_x.at[x],
            device_id=(peer, z, c, t), device_id_type=MESH)
        copy.start()
        sent.append(copy)
    own.wait()
    for k in range(1, n_x):
        peer = lax.rem(x + k, n_x)
        pltpu.make_async_remote_copy(
            src_ref=row_buf, dst_ref=whole_buf.at[span(block(peer, z, c), 1)],
            send_sem=send_x.at[peer], recv_sem=recv_x.at[peer],
            device_id=(peer, z, c, t), device_id_type=MESH).wait_recv()
    for copy in sent:
        copy.wait_send()

    strip = span(block(0, z, c), n_x)
    sent = []
    for k in range(1, n_z):
        peer = lax.rem(z + k, n_z)
        copy = pltpu.make_async_remote_copy(
            src_ref=whole_buf.at[strip], dst_ref=whole_buf.at[strip],
            send_sem=send_z.at[peer], recv_sem=recv_z.at[z],
            device_id=(x, peer, c, t), device_id_type=MESH)
        copy.start()
        sent.append(copy)
    for k in range(1, n_z):
        peer = lax.rem(z + k, n_z)
        other = span(block(0, peer, c), n_x)
        pltpu.make_async_remote_copy(
            src_ref=whole_buf.at[other], dst_ref=whole_buf.at[other],
            send_sem=send_z.at[peer], recv_sem=recv_z.at[peer],
            device_id=(x, peer, c, t), device_id_type=MESH).wait_recv()
    for copy in sent:
        copy.wait_send()

    half = span(block(0, 0, c), n_z * n_x)
    sent = []
    for k in range(1, n_c):
        peer = lax.rem(c + k, n_c)
        copy = pltpu.make_async_remote_copy(
            src_ref=whole_buf.at[half], dst_ref=whole_buf.at[half],
            send_sem=send_c.at[peer], recv_sem=recv_c.at[c],
            device_id=(x, z, peer, t), device_id_type=MESH)
        copy.start()
        sent.append(copy)
    for k in range(1, n_c):
        peer = lax.rem(c + k, n_c)
        other = span(block(0, 0, peer), n_z * n_x)
        pltpu.make_async_remote_copy(
            src_ref=whole_buf.at[other], dst_ref=whole_buf.at[other],
            send_sem=send_c.at[peer], recv_sem=recv_c.at[peer],
            device_id=(x, z, peer, t), device_id_type=MESH).wait_recv()
    for copy in sent:
        copy.wait_send()
    out_ref[...] = whole_buf[...]


def gather3(advance, sizes, n_tensor):
    mats, rows, cols = advance.shape
    n_x, n_z, n_c = sizes
    DMA = pltpu.SemaphoreType.DMA
    return pl.pallas_call(
        functools.partial(gather3_kernel, sizes, n_tensor),
        out_shape=jax.ShapeDtypeStruct((n_x * n_z * n_c * rows, n_tensor * cols), advance.dtype),
        in_specs=[pl.BlockSpec(memory_space=pltpu.VMEM)],
        out_specs=pl.BlockSpec(memory_space=pltpu.VMEM),
        scratch_shapes=[
            pltpu.VMEM((rows, n_tensor * cols), advance.dtype),
            pltpu.VMEM((n_x * n_z * n_c * rows, n_tensor * cols), advance.dtype),
            DMA((n_tensor,)), DMA((n_tensor,)),
            DMA((n_x,)), DMA((n_x,)),
            DMA((n_z,)), DMA((n_z,)),
            DMA((n_c,)), DMA((n_c,)),
            DMA,
        ],
        compiler_params=pltpu.CompilerParams(collective_id=0, has_side_effects=True),
    )(advance)


def scatter_kernel(n_tensor, piece_ref, out_ref, out_buf, send_sem, recv_sem, local_sem):
    here = tuple(lax.axis_index(a) for a in SHARD_AXES)
    t = lax.axis_index("tensor")
    barrier = pltpu.get_barrier_semaphore()
    for k in range(1, n_tensor):
        pl.semaphore_signal(barrier, inc=1, device_id=here + (lax.rem(t + k, n_tensor),),
                            device_id_type=MESH)
    pl.semaphore_wait(barrier, n_tensor - 1)
    own = pltpu.make_async_copy(piece_ref.at[t], out_buf.at[t], local_sem)
    own.start()
    copies = []
    for k in range(1, n_tensor):
        peer = lax.rem(t + k, n_tensor)
        copy = pltpu.make_async_remote_copy(
            src_ref=piece_ref.at[peer], dst_ref=out_buf.at[t],
            send_sem=send_sem.at[peer], recv_sem=recv_sem.at[t],
            device_id=here + (peer,), device_id_type=MESH)
        copy.start()
        copies.append(copy)
    own.wait()
    for k in range(1, n_tensor):
        peer = lax.rem(t + k, n_tensor)
        pltpu.make_async_remote_copy(
            src_ref=piece_ref.at[t], dst_ref=out_buf.at[peer],
            send_sem=send_sem.at[peer], recv_sem=recv_sem.at[peer],
            device_id=here + (peer,), device_id_type=MESH).wait_recv()
        copies[k - 1].wait_send()
    out_ref[...] = out_buf[...]


def scatter(pieces):
    n_tensor = pieces.shape[0]
    return pl.pallas_call(
        functools.partial(scatter_kernel, n_tensor),
        out_shape=jax.ShapeDtypeStruct(pieces.shape, pieces.dtype),
        in_specs=[pl.BlockSpec(memory_space=pltpu.VMEM)],
        out_specs=pl.BlockSpec(memory_space=pltpu.VMEM),
        scratch_shapes=[
            pltpu.VMEM(pieces.shape, pieces.dtype),
            pltpu.SemaphoreType.DMA((n_tensor,)),
            pltpu.SemaphoreType.DMA((n_tensor,)),
            pltpu.SemaphoreType.DMA,
        ],
        compiler_params=pltpu.CompilerParams(collective_id=1, has_side_effects=True),
    )(pieces)


def split_dot(wide_lhs, rhs):
    high = wide_lhs.astype(jnp.bfloat16)
    low = (wide_lhs - high.astype(jnp.float32)).astype(jnp.bfloat16)
    both = jnp.concatenate([high, low], axis=1)
    return jnp.dot(both, jnp.concatenate([rhs, rhs], axis=0), preferred_element_type=jnp.float32)


def polish(iterate, gram, rows=None):
    squared_rows = gram if rows is None else rows(gram)
    squared = jnp.dot(squared_rows, gram, precision=lax.Precision.HIGH)
    poly = second_coef * squared_rows + third_coef * squared
    head = iterate if rows is None else rows(iterate)
    fresh = first_coef * head.astype(jnp.float32) + split_dot(poly, iterate)
    return fresh.astype(jnp.bfloat16)


def on_device(grad, momentum, weight):
    mats, rows_local, cols_local = grad.shape
    n_tensor = lax.axis_size("tensor")
    new_momentum = mu_decay * momentum + grad
    advance = (grad + mu_decay * new_momentum).astype(jnp.bfloat16)
    sizes = tuple(lax.axis_size(axis) for axis in SHARD_AXES)
    whole = gather3(advance, sizes, n_tensor)
    wide = whole.astype(jnp.float32)
    frob = jnp.sqrt(jnp.sum(wide * wide)) + epsilon
    iterate = (wide / frob).astype(jnp.bfloat16)
    block = 0
    for axis in reversed(SHARD_AXES):
        block = block * lax.axis_size(axis) + lax.axis_index(axis)
    start = block * rows_local

    def mine(full):
        return lax.dynamic_slice_in_dim(full, start, rows_local, axis=0)

    for step in range(ITERS):
        gram = jnp.dot(iterate, iterate.T, preferred_element_type=jnp.float32)
        iterate = polish(iterate, gram, mine if step == ITERS - 1 else None)
    pieces = iterate.reshape(rows_local, n_tensor, cols_local).transpose(1, 0, 2)
    ortho = scatter(pieces)
    width = cols_local * n_tensor
    update = update_gain * math.sqrt(width) * ortho.astype(jnp.float32)
    new_weight = weight - learn_rate * (update + weight_decay * weight)
    return (new_weight, new_momentum, update)


def split_shard(mesh):
    devices = mesh.devices
    column = devices[:, 0]
    try:
        n_x = len({d.coords[0] for d in column})
        n_z = len({d.coords[2] for d in column})
        n_core = len({d.core_on_chip for d in column})
    except AttributeError:
        n_x, n_z, n_core = len(column), 1, 1
    if n_x * n_z * n_core != len(column):
        n_x, n_z, n_core = len(column), 1, 1
    grid = devices.reshape(n_x, n_z, n_core, devices.shape[1])
    return jax.sharding.Mesh(grid, SHARD_AXES + ("tensor",))


def solution(mesh):
    fine = split_shard(mesh)
    spec = P(None, SHARD_AXES, "tensor")
    return jax.shard_map(
        on_device, mesh=fine, in_specs=(spec,) * 3, out_specs=(spec,) * 3, check_vma=False
    )
```

```python
import math

import jax
import jax.numpy as jnp
from jax import lax
from jax.experimental import pallas as pl
from jax.experimental.pallas import tpu as pltpu
from jax.sharding import PartitionSpec as P
import functools

ITERS = 3
SHARD_AXES = ("sx", "sz", "sc")


mu_decay = 0.95
learn_rate = 0.05
weight_decay = 0.1
update_gain = 0.2
first_coef = 3.4445
second_coef = -4.775
third_coef = 2.0315
epsilon = 1e-07


MESH = pl.DeviceIdType.MESH


def shard_coords(index, sizes):
    coords = []
    for size in reversed(sizes):
        coords.append(index % size)
        index = index // size
    return tuple(reversed(coords))


def gather3_kernel(sizes, n_tensor, adv_ref, out_ref, square_ref, row_buf, whole_buf,
                   send1, recv1, send_x, recv_x, send_z, recv_z, send_c, recv_c, local_sem):
    mats, rows, cols = adv_ref.shape
    n_x, n_z, n_c = sizes
    x, z, c = (lax.axis_index(a) for a in SHARD_AXES)
    here = (x, z, c)
    t = lax.axis_index("tensor")

    def block(bx, bz, bc):
        return (bc * n_z + bz) * n_x + bx

    def span(first, count):
        return pl.ds(pl.multiple_of(first * rows, rows), count * rows)

    barrier = pltpu.get_barrier_semaphore()
    peers = [here + (lax.rem(t + k, n_tensor),) for k in range(1, n_tensor)]
    peers += [(lax.rem(x + k, n_x), z, c, t) for k in range(1, n_x)]
    peers += [(x, lax.rem(z + k, n_z), c, t) for k in range(1, n_z)]
    peers += [(x, z, lax.rem(c + k, n_c), t) for k in range(1, n_c)]
    for peer in peers:
        pl.semaphore_signal(barrier, inc=1, device_id=peer, device_id_type=MESH)
    pl.semaphore_wait(barrier, len(peers))

    my_cols = pl.ds(pl.multiple_of(t * cols, cols), cols)
    own = pltpu.make_async_copy(adv_ref.at[t], row_buf.at[:, my_cols], local_sem)
    own.start()
    sent = []
    for k in range(1, n_tensor):
        peer = lax.rem(t + k, n_tensor)
        copy = pltpu.make_async_remote_copy(
            src_ref=adv_ref.at[peer], dst_ref=row_buf.at[:, my_cols],
            send_sem=send1.at[peer], recv_sem=recv1.at[t],
            device_id=here + (peer,), device_id_type=MESH)
        copy.start()
        sent.append(copy)
    own.wait()
    for k in range(1, n_tensor):
        peer = lax.rem(t + k, n_tensor)
        peer_cols = pl.ds(pl.multiple_of(peer * cols, cols), cols)
        pltpu.make_async_remote_copy(
            src_ref=adv_ref.at[t], dst_ref=row_buf.at[:, peer_cols],
            send_sem=send1.at[peer], recv_sem=recv1.at[peer],
            device_id=here + (peer,), device_id_type=MESH).wait_recv()
    for copy in sent:
        copy.wait_send()

    mine = span(block(x, z, c), 1)
    own = pltpu.make_async_copy(row_buf, whole_buf.at[mine], local_sem)
    own.start()
    sent = []
    for k in range(1, n_x):
        peer = lax.rem(x + k, n_x)
        copy = pltpu.make_async_remote_copy(
            src_ref=row_buf, dst_ref=whole_buf.at[mine],
            send_sem=send_x.at[peer], recv_sem=recv_x.at[x],
            device_id=(peer, z, c, t), device_id_type=MESH)
        copy.start()
        sent.append(copy)
    own.wait()
    for k in range(1, n_x):
        peer = lax.rem(x + k, n_x)
        pltpu.make_async_remote_copy(
            src_ref=row_buf, dst_ref=whole_buf.at[span(block(peer, z, c), 1)],
            send_sem=send_x.at[peer], recv_sem=recv_x.at[peer],
            device_id=(peer, z, c, t), device_id_type=MESH).wait_recv()
    for copy in sent:
        copy.wait_send()

    strip = span(block(0, z, c), n_x)
    sent = []
    for k in range(1, n_z):
        peer = lax.rem(z + k, n_z)
        copy = pltpu.make_async_remote_copy(
            src_ref=whole_buf.at[strip], dst_ref=whole_buf.at[strip],
            send_sem=send_z.at[peer], recv_sem=recv_z.at[z],
            device_id=(x, peer, c, t), device_id_type=MESH)
        copy.start()
        sent.append(copy)
    for k in range(1, n_z):
        peer = lax.rem(z + k, n_z)
        other = span(block(0, peer, c), n_x)
        pltpu.make_async_remote_copy(
            src_ref=whole_buf.at[other], dst_ref=whole_buf.at[other],
            send_sem=send_z.at[peer], recv_sem=recv_z.at[peer],
            device_id=(x, peer, c, t), device_id_type=MESH).wait_recv()
    for copy in sent:
        copy.wait_send()

    half = span(block(0, 0, c), n_z * n_x)
    sent = []
    for k in range(1, n_c):
        peer = lax.rem(c + k, n_c)
        copy = pltpu.make_async_remote_copy(
            src_ref=whole_buf.at[half], dst_ref=whole_buf.at[half],
            send_sem=send_c.at[peer], recv_sem=recv_c.at[c],
            device_id=(x, z, peer, t), device_id_type=MESH)
        copy.start()
        sent.append(copy)
    for k in range(1, n_c):
        peer = lax.rem(c + k, n_c)
        other = span(block(0, 0, peer), n_z * n_x)
        pltpu.make_async_remote_copy(
            src_ref=whole_buf.at[other], dst_ref=whole_buf.at[other],
            send_sem=send_c.at[peer], recv_sem=recv_c.at[peer],
            device_id=(x, z, peer, t), device_id_type=MESH).wait_recv()
    for copy in sent:
        copy.wait_send()
    out_ref[...] = whole_buf[...]

    def square(i, total):
        piece = whole_buf[pl.ds(pl.multiple_of(i * rows, rows), rows), :].astype(jnp.float32)
        return total + piece * piece

    total = lax.fori_loop(0, n_x * n_z * n_c, square,
                          jnp.zeros((rows, n_tensor * cols), jnp.float32))
    square_ref[...] = jnp.broadcast_to(jnp.sum(total), square_ref.shape)


def gather3(advance, sizes, n_tensor):
    mats, rows, cols = advance.shape
    n_x, n_z, n_c = sizes
    DMA = pltpu.SemaphoreType.DMA
    return pl.pallas_call(
        functools.partial(gather3_kernel, sizes, n_tensor),
        out_shape=(
            jax.ShapeDtypeStruct((n_x * n_z * n_c * rows, n_tensor * cols), advance.dtype),
            jax.ShapeDtypeStruct((8, 128), jnp.float32),
        ),
        in_specs=[pl.BlockSpec(memory_space=pltpu.VMEM)],
        out_specs=(pl.BlockSpec(memory_space=pltpu.VMEM), pl.BlockSpec(memory_space=pltpu.VMEM)),
        scratch_shapes=[
            pltpu.VMEM((rows, n_tensor * cols), advance.dtype),
            pltpu.VMEM((n_x * n_z * n_c * rows, n_tensor * cols), advance.dtype),
            DMA((n_tensor,)), DMA((n_tensor,)),
            DMA((n_x,)), DMA((n_x,)),
            DMA((n_z,)), DMA((n_z,)),
            DMA((n_c,)), DMA((n_c,)),
            DMA,
        ],
        compiler_params=pltpu.CompilerParams(collective_id=0, has_side_effects=True),
    )(advance)


def scatter_kernel(n_tensor, piece_ref, out_ref, out_buf, send_sem, recv_sem, local_sem):
    here = tuple(lax.axis_index(a) for a in SHARD_AXES)
    t = lax.axis_index("tensor")
    barrier = pltpu.get_barrier_semaphore()
    for k in range(1, n_tensor):
        pl.semaphore_signal(barrier, inc=1, device_id=here + (lax.rem(t + k, n_tensor),),
                            device_id_type=MESH)
    pl.semaphore_wait(barrier, n_tensor - 1)
    own = pltpu.make_async_copy(piece_ref.at[t], out_buf.at[t], local_sem)
    own.start()
    copies = []
    for k in range(1, n_tensor):
        peer = lax.rem(t + k, n_tensor)
        copy = pltpu.make_async_remote_copy(
            src_ref=piece_ref.at[peer], dst_ref=out_buf.at[t],
            send_sem=send_sem.at[peer], recv_sem=recv_sem.at[t],
            device_id=here + (peer,), device_id_type=MESH)
        copy.start()
        copies.append(copy)
    own.wait()
    for k in range(1, n_tensor):
        peer = lax.rem(t + k, n_tensor)
        pltpu.make_async_remote_copy(
            src_ref=piece_ref.at[t], dst_ref=out_buf.at[peer],
            send_sem=send_sem.at[peer], recv_sem=recv_sem.at[peer],
            device_id=here + (peer,), device_id_type=MESH).wait_recv()
        copies[k - 1].wait_send()
    out_ref[...] = out_buf[...]


def scatter(pieces):
    n_tensor = pieces.shape[0]
    return pl.pallas_call(
        functools.partial(scatter_kernel, n_tensor),
        out_shape=jax.ShapeDtypeStruct(pieces.shape, pieces.dtype),
        in_specs=[pl.BlockSpec(memory_space=pltpu.VMEM)],
        out_specs=pl.BlockSpec(memory_space=pltpu.VMEM),
        scratch_shapes=[
            pltpu.VMEM(pieces.shape, pieces.dtype),
            pltpu.SemaphoreType.DMA((n_tensor,)),
            pltpu.SemaphoreType.DMA((n_tensor,)),
            pltpu.SemaphoreType.DMA,
        ],
        compiler_params=pltpu.CompilerParams(collective_id=1, has_side_effects=True),
    )(pieces)


def split_dot(wide_lhs, rhs):
    high = wide_lhs.astype(jnp.bfloat16)
    low = (wide_lhs - high.astype(jnp.float32)).astype(jnp.bfloat16)
    both = jnp.concatenate([high, low], axis=1)
    return jnp.dot(both, jnp.concatenate([rhs, rhs], axis=0), preferred_element_type=jnp.float32)


def polish(iterate, gram, rows=None):
    squared_rows = gram if rows is None else rows(gram)
    squared = jnp.dot(squared_rows, gram, precision=lax.Precision.HIGH)
    poly = second_coef * squared_rows + third_coef * squared
    head = iterate if rows is None else rows(iterate)
    fresh = first_coef * head.astype(jnp.float32) + split_dot(poly, iterate)
    return fresh.astype(jnp.bfloat16)


def on_device(grad, momentum, weight):
    mats, rows_local, cols_local = grad.shape
    n_tensor = lax.axis_size("tensor")
    new_momentum = mu_decay * momentum + grad
    advance = (grad + mu_decay * new_momentum).astype(jnp.bfloat16)
    sizes = tuple(lax.axis_size(axis) for axis in SHARD_AXES)
    whole, squares = gather3(advance, sizes, n_tensor)
    wide = whole.astype(jnp.float32)
    frob = jnp.sqrt(squares[0, 0]) + epsilon
    iterate = (wide / frob).astype(jnp.bfloat16)
    block = 0
    for axis in reversed(SHARD_AXES):
        block = block * lax.axis_size(axis) + lax.axis_index(axis)
    start = block * rows_local

    def mine(full):
        return lax.dynamic_slice_in_dim(full, start, rows_local, axis=0)

    for step in range(ITERS):
        gram = jnp.dot(iterate, iterate.T, preferred_element_type=jnp.float32)
        iterate = polish(iterate, gram, mine if step == ITERS - 1 else None)
    pieces = iterate.reshape(rows_local, n_tensor, cols_local).transpose(1, 0, 2)
    ortho = scatter(pieces)
    width = cols_local * n_tensor
    update = update_gain * math.sqrt(width) * ortho.astype(jnp.float32)
    new_weight = weight - learn_rate * (update + weight_decay * weight)
    return (new_weight, new_momentum, update)


def split_shard(mesh):
    devices = mesh.devices
    column = devices[:, 0]
    try:
        n_x = len({d.coords[0] for d in column})
        n_z = len({d.coords[2] for d in column})
        n_core = len({d.core_on_chip for d in column})
    except AttributeError:
        n_x, n_z, n_core = len(column), 1, 1
    if n_x * n_z * n_core != len(column):
        n_x, n_z, n_core = len(column), 1, 1
    grid = devices.reshape(n_x, n_z, n_core, devices.shape[1])
    return jax.sharding.Mesh(grid, SHARD_AXES + ("tensor",))


def solution(mesh):
    fine = split_shard(mesh)
    spec = P(None, SHARD_AXES, "tensor")
    return jax.shard_map(
        on_device, mesh=fine, in_specs=(spec,) * 3, out_specs=(spec,) * 3, check_vma=False
    )
```

```python
import math

import jax
import jax.numpy as jnp
from jax import lax
from jax.experimental import pallas as pl
from jax.experimental.pallas import tpu as pltpu
from jax.sharding import PartitionSpec as P
import functools

ITERS = 3
SHARD_AXES = ("sx", "sz", "sc")


mu_decay = 0.95
learn_rate = 0.05
weight_decay = 0.1
update_gain = 0.2
first_coef = 3.4445
second_coef = -4.775
third_coef = 2.0315
epsilon = 1e-07


MESH = pl.DeviceIdType.MESH


def shard_coords(index, sizes):
    coords = []
    for size in reversed(sizes):
        coords.append(index % size)
        index = index // size
    return tuple(reversed(coords))


def gather3_kernel(sizes, n_tensor, adv_ref, out_ref, square_ref, row_buf, whole_buf,
                   send1, recv1, send_x, recv_x, send_z, recv_z, send_c, recv_c, local_sem):
    mats, rows, cols = adv_ref.shape
    n_x, n_z, n_c = sizes
    x, z, c = (lax.axis_index(a) for a in SHARD_AXES)
    here = (x, z, c)
    t = lax.axis_index("tensor")

    def block(bx, bz, bc):
        return (bc * n_z + bz) * n_x + bx

    def span(first, count):
        return pl.ds(pl.multiple_of(first * rows, rows), count * rows)

    barrier = pltpu.get_barrier_semaphore()
    peers = [here + (lax.rem(t + k, n_tensor),) for k in range(1, n_tensor)]
    peers += [(lax.rem(x + k, n_x), z, c, t) for k in range(1, n_x)]
    peers += [(x, lax.rem(z + k, n_z), c, t) for k in range(1, n_z)]
    peers += [(x, z, lax.rem(c + k, n_c), t) for k in range(1, n_c)]
    for peer in peers:
        pl.semaphore_signal(barrier, inc=1, device_id=peer, device_id_type=MESH)
    pl.semaphore_wait(barrier, len(peers))

    my_cols = pl.ds(pl.multiple_of(t * cols, cols), cols)
    own = pltpu.make_async_copy(adv_ref.at[t], row_buf.at[:, my_cols], local_sem)
    own.start()
    sent = []
    for k in range(1, n_tensor):
        peer = lax.rem(t + k, n_tensor)
        copy = pltpu.make_async_remote_copy(
            src_ref=adv_ref.at[peer], dst_ref=row_buf.at[:, my_cols],
            send_sem=send1.at[peer], recv_sem=recv1.at[t],
            device_id=here + (peer,), device_id_type=MESH)
        copy.start()
        sent.append(copy)
    own.wait()
    for k in range(1, n_tensor):
        peer = lax.rem(t + k, n_tensor)
        peer_cols = pl.ds(pl.multiple_of(peer * cols, cols), cols)
        pltpu.make_async_remote_copy(
            src_ref=adv_ref.at[t], dst_ref=row_buf.at[:, peer_cols],
            send_sem=send1.at[peer], recv_sem=recv1.at[peer],
            device_id=here + (peer,), device_id_type=MESH).wait_recv()
    for copy in sent:
        copy.wait_send()

    mine = span(block(x, z, c), 1)
    own = pltpu.make_async_copy(row_buf, whole_buf.at[mine], local_sem)
    own.start()
    sent = []
    for k in range(1, n_x):
        peer = lax.rem(x + k, n_x)
        copy = pltpu.make_async_remote_copy(
            src_ref=row_buf, dst_ref=whole_buf.at[mine],
            send_sem=send_x.at[peer], recv_sem=recv_x.at[x],
            device_id=(peer, z, c, t), device_id_type=MESH)
        copy.start()
        sent.append(copy)
    own.wait()
    for k in range(1, n_x):
        peer = lax.rem(x + k, n_x)
        pltpu.make_async_remote_copy(
            src_ref=row_buf, dst_ref=whole_buf.at[span(block(peer, z, c), 1)],
            send_sem=send_x.at[peer], recv_sem=recv_x.at[peer],
            device_id=(peer, z, c, t), device_id_type=MESH).wait_recv()
    for copy in sent:
        copy.wait_send()

    strip = span(block(0, z, c), n_x)
    sent = []
    for k in range(1, n_z):
        peer = lax.rem(z + k, n_z)
        copy = pltpu.make_async_remote_copy(
            src_ref=whole_buf.at[strip], dst_ref=whole_buf.at[strip],
            send_sem=send_z.at[peer], recv_sem=recv_z.at[z],
            device_id=(x, peer, c, t), device_id_type=MESH)
        copy.start()
        sent.append(copy)
    for k in range(1, n_z):
        peer = lax.rem(z + k, n_z)
        other = span(block(0, peer, c), n_x)
        pltpu.make_async_remote_copy(
            src_ref=whole_buf.at[other], dst_ref=whole_buf.at[other],
            send_sem=send_z.at[peer], recv_sem=recv_z.at[peer],
            device_id=(x, peer, c, t), device_id_type=MESH).wait_recv()
    for copy in sent:
        copy.wait_send()

    half = span(block(0, 0, c), n_z * n_x)
    sent = []
    for k in range(1, n_c):
        peer = lax.rem(c + k, n_c)
        copy = pltpu.make_async_remote_copy(
            src_ref=whole_buf.at[half], dst_ref=whole_buf.at[half],
            send_sem=send_c.at[peer], recv_sem=recv_c.at[c],
            device_id=(x, z, peer, t), device_id_type=MESH)
        copy.start()
        sent.append(copy)
    for k in range(1, n_c):
        peer = lax.rem(c + k, n_c)
        other = span(block(0, 0, peer), n_z * n_x)
        pltpu.make_async_remote_copy(
            src_ref=whole_buf.at[other], dst_ref=whole_buf.at[other],
            send_sem=send_c.at[peer], recv_sem=recv_c.at[peer],
            device_id=(x, z, peer, t), device_id_type=MESH).wait_recv()
    for copy in sent:
        copy.wait_send()
    out_ref[...] = whole_buf[...]

    def square(i, total):
        piece = whole_buf[pl.ds(pl.multiple_of(i * rows, rows), rows), :].astype(jnp.float32)
        return total + piece * piece

    total = lax.fori_loop(0, n_x * n_z * n_c, square,
                          jnp.zeros((rows, n_tensor * cols), jnp.float32))
    square_ref[...] = jnp.broadcast_to(jnp.sum(total), square_ref.shape)


def gather3(advance, sizes, n_tensor):
    mats, rows, cols = advance.shape
    n_x, n_z, n_c = sizes
    DMA = pltpu.SemaphoreType.DMA
    return pl.pallas_call(
        functools.partial(gather3_kernel, sizes, n_tensor),
        out_shape=(
            jax.ShapeDtypeStruct((n_x * n_z * n_c * rows, n_tensor * cols), advance.dtype),
            jax.ShapeDtypeStruct((8, 128), jnp.float32),
        ),
        in_specs=[pl.BlockSpec(memory_space=pltpu.VMEM)],
        out_specs=(pl.BlockSpec(memory_space=pltpu.VMEM), pl.BlockSpec(memory_space=pltpu.VMEM)),
        scratch_shapes=[
            pltpu.VMEM((rows, n_tensor * cols), advance.dtype),
            pltpu.VMEM((n_x * n_z * n_c * rows, n_tensor * cols), advance.dtype),
            DMA((n_tensor,)), DMA((n_tensor,)),
            DMA((n_x,)), DMA((n_x,)),
            DMA((n_z,)), DMA((n_z,)),
            DMA((n_c,)), DMA((n_c,)),
            DMA,
        ],
        compiler_params=pltpu.CompilerParams(collective_id=0, has_side_effects=True),
    )(advance)


def scatter_kernel(n_tensor, piece_ref, out_ref, out_buf, send_sem, recv_sem, local_sem):
    here = tuple(lax.axis_index(a) for a in SHARD_AXES)
    t = lax.axis_index("tensor")
    barrier = pltpu.get_barrier_semaphore()
    for k in range(1, n_tensor):
        pl.semaphore_signal(barrier, inc=1, device_id=here + (lax.rem(t + k, n_tensor),),
                            device_id_type=MESH)
    pl.semaphore_wait(barrier, n_tensor - 1)
    own = pltpu.make_async_copy(piece_ref.at[t], out_buf.at[t], local_sem)
    own.start()
    copies = []
    for k in range(1, n_tensor):
        peer = lax.rem(t + k, n_tensor)
        copy = pltpu.make_async_remote_copy(
            src_ref=piece_ref.at[peer], dst_ref=out_buf.at[t],
            send_sem=send_sem.at[peer], recv_sem=recv_sem.at[t],
            device_id=here + (peer,), device_id_type=MESH)
        copy.start()
        copies.append(copy)
    own.wait()
    for k in range(1, n_tensor):
        peer = lax.rem(t + k, n_tensor)
        pltpu.make_async_remote_copy(
            src_ref=piece_ref.at[t], dst_ref=out_buf.at[peer],
            send_sem=send_sem.at[peer], recv_sem=recv_sem.at[peer],
            device_id=here + (peer,), device_id_type=MESH).wait_recv()
        copies[k - 1].wait_send()
    out_ref[...] = out_buf[...]


def scatter(pieces):
    n_tensor = pieces.shape[0]
    return pl.pallas_call(
        functools.partial(scatter_kernel, n_tensor),
        out_shape=jax.ShapeDtypeStruct(pieces.shape, pieces.dtype),
        in_specs=[pl.BlockSpec(memory_space=pltpu.VMEM)],
        out_specs=pl.BlockSpec(memory_space=pltpu.VMEM),
        scratch_shapes=[
            pltpu.VMEM(pieces.shape, pieces.dtype),
            pltpu.SemaphoreType.DMA((n_tensor,)),
            pltpu.SemaphoreType.DMA((n_tensor,)),
            pltpu.SemaphoreType.DMA,
        ],
        compiler_params=pltpu.CompilerParams(collective_id=1, has_side_effects=True),
    )(pieces)


def split_dot(wide_lhs, rhs):
    high = wide_lhs.astype(jnp.bfloat16)
    low = (wide_lhs - high.astype(jnp.float32)).astype(jnp.bfloat16)
    both = jnp.concatenate([high, low], axis=1)
    return jnp.dot(both, jnp.concatenate([rhs, rhs], axis=0), preferred_element_type=jnp.float32)


def polish(iterate, gram, rows=None):
    squared_rows = gram if rows is None else rows(gram)
    squared = jnp.dot(squared_rows, gram, precision=lax.Precision.HIGH)
    poly = second_coef * squared_rows + third_coef * squared
    head = iterate if rows is None else rows(iterate)
    fresh = first_coef * head.astype(jnp.float32) + split_dot(poly, iterate)
    return fresh.astype(jnp.bfloat16)


def two_part(wide):
    high = wide.astype(jnp.bfloat16)
    return high, (wide - high.astype(jnp.float32)).astype(jnp.bfloat16)


def finish_kernel(sizes, n_tensor, x_ref, out_ref, piece_buf, out_buf, send_sem, recv_sem, local_sem):
    n_x, n_z, n_c = sizes
    x, z, c = (lax.axis_index(a) for a in SHARD_AXES)
    here = (x, z, c)
    t = lax.axis_index("tensor")
    _, rows, cols = piece_buf.shape
    barrier = pltpu.get_barrier_semaphore()
    for k in range(1, n_tensor):
        pl.semaphore_signal(barrier, inc=1, device_id=here + (lax.rem(t + k, n_tensor),),
                            device_id_type=MESH)
    block = (c * n_z + z) * n_x + x
    head = x_ref[pl.ds(pl.multiple_of(block * rows, rows), rows), :]
    full = x_ref[...]
    by_rows = (((1,), (1,)), ((), ()))
    gram = lax.dot_general(head, full, by_rows, preferred_element_type=jnp.float32)
    high, low = two_part(gram)
    across = (jnp.dot(high, full, preferred_element_type=jnp.float32)
              + jnp.dot(low, full, preferred_element_type=jnp.float32))
    high, low = two_part(across)
    squared = (lax.dot_general(high, full, by_rows, preferred_element_type=jnp.float32)
               + lax.dot_general(low, full, by_rows, preferred_element_type=jnp.float32))
    poly = second_coef * gram + third_coef * squared
    high, low = two_part(poly)
    mixed = (jnp.dot(high, full, preferred_element_type=jnp.float32)
             + jnp.dot(low, full, preferred_element_type=jnp.float32))
    fresh = (first_coef * head.astype(jnp.float32) + mixed).astype(jnp.bfloat16)
    for j in range(n_tensor):
        piece_buf[j] = fresh[:, j * cols:(j + 1) * cols]
    pl.semaphore_wait(barrier, n_tensor - 1)
    own = pltpu.make_async_copy(piece_buf.at[t], out_buf.at[t], local_sem)
    own.start()
    copies = []
    for k in range(1, n_tensor):
        peer = lax.rem(t + k, n_tensor)
        copy = pltpu.make_async_remote_copy(
            src_ref=piece_buf.at[peer], dst_ref=out_buf.at[t],
            send_sem=send_sem.at[peer], recv_sem=recv_sem.at[t],
            device_id=here + (peer,), device_id_type=MESH)
        copy.start()
        copies.append(copy)
    own.wait()
    for k in range(1, n_tensor):
        peer = lax.rem(t + k, n_tensor)
        pltpu.make_async_remote_copy(
            src_ref=piece_buf.at[t], dst_ref=out_buf.at[peer],
            send_sem=send_sem.at[peer], recv_sem=recv_sem.at[peer],
            device_id=here + (peer,), device_id_type=MESH).wait_recv()
        copies[k - 1].wait_send()
    out_ref[...] = out_buf[...]


def finish(iterate, sizes, n_tensor, rows):
    cols = iterate.shape[1] // n_tensor
    shape = (n_tensor, rows, cols)
    return pl.pallas_call(
        functools.partial(finish_kernel, sizes, n_tensor),
        out_shape=jax.ShapeDtypeStruct(shape, iterate.dtype),
        in_specs=[pl.BlockSpec(memory_space=pltpu.VMEM)],
        out_specs=pl.BlockSpec(memory_space=pltpu.VMEM),
        scratch_shapes=[
            pltpu.VMEM(shape, iterate.dtype),
            pltpu.VMEM(shape, iterate.dtype),
            pltpu.SemaphoreType.DMA((n_tensor,)),
            pltpu.SemaphoreType.DMA((n_tensor,)),
            pltpu.SemaphoreType.DMA,
        ],
        compiler_params=pltpu.CompilerParams(collective_id=1, has_side_effects=True),
    )(iterate)


def on_device(grad, momentum, weight):
    mats, rows_local, cols_local = grad.shape
    n_tensor = lax.axis_size("tensor")
    new_momentum = mu_decay * momentum + grad
    advance = (grad + mu_decay * new_momentum).astype(jnp.bfloat16)
    sizes = tuple(lax.axis_size(axis) for axis in SHARD_AXES)
    whole, squares = gather3(advance, sizes, n_tensor)
    wide = whole.astype(jnp.float32)
    frob = jnp.sqrt(squares[0, 0]) + epsilon
    iterate = (wide / frob).astype(jnp.bfloat16)
    block = 0
    for axis in reversed(SHARD_AXES):
        block = block * lax.axis_size(axis) + lax.axis_index(axis)
    start = block * rows_local

    def mine(full):
        return lax.dynamic_slice_in_dim(full, start, rows_local, axis=0)

    for step in range(ITERS - 1):
        gram = jnp.dot(iterate, iterate.T, preferred_element_type=jnp.float32)
        iterate = polish(iterate, gram)
    ortho = finish(iterate, sizes, n_tensor, rows_local)
    width = cols_local * n_tensor
    update = update_gain * math.sqrt(width) * ortho.astype(jnp.float32)
    new_weight = weight - learn_rate * (update + weight_decay * weight)
    return (new_weight, new_momentum, update)


def split_shard(mesh):
    devices = mesh.devices
    column = devices[:, 0]
    try:
        n_x = len({d.coords[0] for d in column})
        n_z = len({d.coords[2] for d in column})
        n_core = len({d.core_on_chip for d in column})
    except AttributeError:
        n_x, n_z, n_core = len(column), 1, 1
    if n_x * n_z * n_core != len(column):
        n_x, n_z, n_core = len(column), 1, 1
    grid = devices.reshape(n_x, n_z, n_core, devices.shape[1])
    return jax.sharding.Mesh(grid, SHARD_AXES + ("tensor",))


def solution(mesh):
    fine = split_shard(mesh)
    spec = P(None, SHARD_AXES, "tensor")
    return jax.shard_map(
        on_device, mesh=fine, in_specs=(spec,) * 3, out_specs=(spec,) * 3, check_vma=False
    )
```

```python
import math

import jax
import jax.numpy as jnp
from jax import lax
from jax.experimental import pallas as pl
from jax.experimental.pallas import tpu as pltpu
from jax.sharding import PartitionSpec as P
import functools

ITERS = 3
SHARD_AXES = ("sx", "sz", "sc")


mu_decay = 0.95
learn_rate = 0.05
weight_decay = 0.1
update_gain = 0.2
first_coef = 3.4445
second_coef = -4.775
third_coef = 2.0315
epsilon = 1e-07


MESH = pl.DeviceIdType.MESH


def shard_coords(index, sizes):
    coords = []
    for size in reversed(sizes):
        coords.append(index % size)
        index = index // size
    return tuple(reversed(coords))


def gather3_kernel(sizes, n_tensor, grad_ref, momentum_ref, out_ref, momentum_out,
                   adv_ref, row_buf, whole_buf,
                   send1, recv1, send_x, recv_x, send_z, recv_z, send_c, recv_c, local_sem):
    mats, rows, cols = adv_ref.shape
    n_x, n_z, n_c = sizes
    x, z, c = (lax.axis_index(a) for a in SHARD_AXES)
    here = (x, z, c)
    t = lax.axis_index("tensor")

    def block(bx, bz, bc):
        return (bc * n_z + bz) * n_x + bx

    def span(first, count):
        return pl.ds(pl.multiple_of(first * rows, rows), count * rows)

    barrier = pltpu.get_barrier_semaphore()
    peers = [here + (lax.rem(t + k, n_tensor),) for k in range(1, n_tensor)]
    peers += [(lax.rem(x + k, n_x), z, c, t) for k in range(1, n_x)]
    peers += [(x, lax.rem(z + k, n_z), c, t) for k in range(1, n_z)]
    peers += [(x, z, lax.rem(c + k, n_c), t) for k in range(1, n_c)]
    for peer in peers:
        pl.semaphore_signal(barrier, inc=1, device_id=peer, device_id_type=MESH)
    fresh = mu_decay * momentum_ref[...] + grad_ref[...]
    momentum_out[...] = fresh
    adv_ref[...] = (grad_ref[...] + mu_decay * fresh).astype(adv_ref.dtype)
    pl.semaphore_wait(barrier, len(peers))

    my_cols = pl.ds(pl.multiple_of(t * cols, cols), cols)
    own = pltpu.make_async_copy(adv_ref.at[t], row_buf.at[:, my_cols], local_sem)
    own.start()
    sent = []
    for k in range(1, n_tensor):
        peer = lax.rem(t + k, n_tensor)
        copy = pltpu.make_async_remote_copy(
            src_ref=adv_ref.at[peer], dst_ref=row_buf.at[:, my_cols],
            send_sem=send1.at[peer], recv_sem=recv1.at[t],
            device_id=here + (peer,), device_id_type=MESH)
        copy.start()
        sent.append(copy)
    own.wait()
    for k in range(1, n_tensor):
        peer = lax.rem(t + k, n_tensor)
        peer_cols = pl.ds(pl.multiple_of(peer * cols, cols), cols)
        pltpu.make_async_remote_copy(
            src_ref=adv_ref.at[t], dst_ref=row_buf.at[:, peer_cols],
            send_sem=send1.at[peer], recv_sem=recv1.at[peer],
            device_id=here + (peer,), device_id_type=MESH).wait_recv()
    for copy in sent:
        copy.wait_send()

    mine = span(block(x, z, c), 1)
    own = pltpu.make_async_copy(row_buf, whole_buf.at[mine], local_sem)
    own.start()
    sent = []
    for k in range(1, n_x):
        peer = lax.rem(x + k, n_x)
        copy = pltpu.make_async_remote_copy(
            src_ref=row_buf, dst_ref=whole_buf.at[mine],
            send_sem=send_x.at[peer], recv_sem=recv_x.at[x],
            device_id=(peer, z, c, t), device_id_type=MESH)
        copy.start()
        sent.append(copy)
    own.wait()
    for k in range(1, n_x):
        peer = lax.rem(x + k, n_x)
        pltpu.make_async_remote_copy(
            src_ref=row_buf, dst_ref=whole_buf.at[span(block(peer, z, c), 1)],
            send_sem=send_x.at[peer], recv_sem=recv_x.at[peer],
            device_id=(peer, z, c, t), device_id_type=MESH).wait_recv()
    for copy in sent:
        copy.wait_send()

    strip = span(block(0, z, c), n_x)
    sent = []
    for k in range(1, n_z):
        peer = lax.rem(z + k, n_z)
        copy = pltpu.make_async_remote_copy(
            src_ref=whole_buf.at[strip], dst_ref=whole_buf.at[strip],
            send_sem=send_z.at[peer], recv_sem=recv_z.at[z],
            device_id=(x, peer, c, t), device_id_type=MESH)
        copy.start()
        sent.append(copy)
    for k in range(1, n_z):
        peer = lax.rem(z + k, n_z)
        other = span(block(0, peer, c), n_x)
        pltpu.make_async_remote_copy(
            src_ref=whole_buf.at[other], dst_ref=whole_buf.at[other],
            send_sem=send_z.at[peer], recv_sem=recv_z.at[peer],
            device_id=(x, peer, c, t), device_id_type=MESH).wait_recv()
    for copy in sent:
        copy.wait_send()

    half = span(block(0, 0, c), n_z * n_x)
    sent = []
    for k in range(1, n_c):
        peer = lax.rem(c + k, n_c)
        copy = pltpu.make_async_remote_copy(
            src_ref=whole_buf.at[half], dst_ref=whole_buf.at[half],
            send_sem=send_c.at[peer], recv_sem=recv_c.at[c],
            device_id=(x, z, peer, t), device_id_type=MESH)
        copy.start()
        sent.append(copy)
    for k in range(1, n_c):
        peer = lax.rem(c + k, n_c)
        other = span(block(0, 0, peer), n_z * n_x)
        pltpu.make_async_remote_copy(
            src_ref=whole_buf.at[other], dst_ref=whole_buf.at[other],
            send_sem=send_c.at[peer], recv_sem=recv_c.at[peer],
            device_id=(x, z, peer, t), device_id_type=MESH).wait_recv()
    for copy in sent:
        copy.wait_send()

    def square(i, total):
        piece = whole_buf[pl.ds(pl.multiple_of(i * rows, rows), rows), :].astype(jnp.float32)
        return total + piece * piece

    total = lax.fori_loop(0, n_x * n_z * n_c, square,
                          jnp.zeros((rows, n_tensor * cols), jnp.float32))
    frob = jnp.sqrt(jnp.sum(total, keepdims=True)) + epsilon

    def scale(i, carry):
        band = pl.ds(pl.multiple_of(i * rows, rows), rows)
        out_ref[band, :] = (whole_buf[band, :].astype(jnp.float32) / frob).astype(out_ref.dtype)
        return carry

    lax.fori_loop(0, n_x * n_z * n_c, scale, 0)


def gather3(grad, momentum, sizes, n_tensor):
    mats, rows, cols = grad.shape
    n_x, n_z, n_c = sizes
    DMA = pltpu.SemaphoreType.DMA
    vmem = pl.BlockSpec(memory_space=pltpu.VMEM)
    return pl.pallas_call(
        functools.partial(gather3_kernel, sizes, n_tensor),
        out_shape=(
            jax.ShapeDtypeStruct((n_x * n_z * n_c * rows, n_tensor * cols), jnp.bfloat16),
            jax.ShapeDtypeStruct(momentum.shape, momentum.dtype),
        ),
        in_specs=[vmem, vmem],
        out_specs=(vmem, vmem),
        scratch_shapes=[
            pltpu.VMEM((mats, rows, cols), jnp.bfloat16),
            pltpu.VMEM((rows, n_tensor * cols), jnp.bfloat16),
            pltpu.VMEM((n_x * n_z * n_c * rows, n_tensor * cols), jnp.bfloat16),
            DMA((n_tensor,)), DMA((n_tensor,)),
            DMA((n_x,)), DMA((n_x,)),
            DMA((n_z,)), DMA((n_z,)),
            DMA((n_c,)), DMA((n_c,)),
            DMA,
        ],
        compiler_params=pltpu.CompilerParams(collective_id=0, has_side_effects=True),
    )(grad, momentum)


def scatter_kernel(n_tensor, piece_ref, out_ref, out_buf, send_sem, recv_sem, local_sem):
    here = tuple(lax.axis_index(a) for a in SHARD_AXES)
    t = lax.axis_index("tensor")
    barrier = pltpu.get_barrier_semaphore()
    for k in range(1, n_tensor):
        pl.semaphore_signal(barrier, inc=1, device_id=here + (lax.rem(t + k, n_tensor),),
                            device_id_type=MESH)
    pl.semaphore_wait(barrier, n_tensor - 1)
    own = pltpu.make_async_copy(piece_ref.at[t], out_buf.at[t], local_sem)
    own.start()
    copies = []
    for k in range(1, n_tensor):
        peer = lax.rem(t + k, n_tensor)
        copy = pltpu.make_async_remote_copy(
            src_ref=piece_ref.at[peer], dst_ref=out_buf.at[t],
            send_sem=send_sem.at[peer], recv_sem=recv_sem.at[t],
            device_id=here + (peer,), device_id_type=MESH)
        copy.start()
        copies.append(copy)
    own.wait()
    for k in range(1, n_tensor):
        peer = lax.rem(t + k, n_tensor)
        pltpu.make_async_remote_copy(
            src_ref=piece_ref.at[t], dst_ref=out_buf.at[peer],
            send_sem=send_sem.at[peer], recv_sem=recv_sem.at[peer],
            device_id=here + (peer,), device_id_type=MESH).wait_recv()
        copies[k - 1].wait_send()
    out_ref[...] = out_buf[...]


def scatter(pieces):
    n_tensor = pieces.shape[0]
    return pl.pallas_call(
        functools.partial(scatter_kernel, n_tensor),
        out_shape=jax.ShapeDtypeStruct(pieces.shape, pieces.dtype),
        in_specs=[pl.BlockSpec(memory_space=pltpu.VMEM)],
        out_specs=pl.BlockSpec(memory_space=pltpu.VMEM),
        scratch_shapes=[
            pltpu.VMEM(pieces.shape, pieces.dtype),
            pltpu.SemaphoreType.DMA((n_tensor,)),
            pltpu.SemaphoreType.DMA((n_tensor,)),
            pltpu.SemaphoreType.DMA,
        ],
        compiler_params=pltpu.CompilerParams(collective_id=1, has_side_effects=True),
    )(pieces)


def split_dot(wide_lhs, rhs):
    high = wide_lhs.astype(jnp.bfloat16)
    low = (wide_lhs - high.astype(jnp.float32)).astype(jnp.bfloat16)
    both = jnp.concatenate([high, low], axis=1)
    return jnp.dot(both, jnp.concatenate([rhs, rhs], axis=0), preferred_element_type=jnp.float32)


def polish(iterate, gram, rows=None):
    squared_rows = gram if rows is None else rows(gram)
    squared = jnp.dot(squared_rows, gram, precision=lax.Precision.HIGH)
    poly = second_coef * squared_rows + third_coef * squared
    head = iterate if rows is None else rows(iterate)
    fresh = first_coef * head.astype(jnp.float32) + split_dot(poly, iterate)
    return fresh.astype(jnp.bfloat16)


def two_part(wide):
    high = wide.astype(jnp.bfloat16)
    return high, (wide - high.astype(jnp.float32)).astype(jnp.bfloat16)


def finish_kernel(sizes, n_tensor, x_ref, weight_ref, update_ref, weight_out,
                  piece_buf, out_buf, send_sem, recv_sem, local_sem):
    n_x, n_z, n_c = sizes
    x, z, c = (lax.axis_index(a) for a in SHARD_AXES)
    here = (x, z, c)
    t = lax.axis_index("tensor")
    _, rows, cols = piece_buf.shape
    barrier = pltpu.get_barrier_semaphore()
    for k in range(1, n_tensor):
        pl.semaphore_signal(barrier, inc=1, device_id=here + (lax.rem(t + k, n_tensor),),
                            device_id_type=MESH)
    block = (c * n_z + z) * n_x + x
    head = x_ref[pl.ds(pl.multiple_of(block * rows, rows), rows), :]
    full = x_ref[...]
    by_rows = (((1,), (1,)), ((), ()))
    gram = lax.dot_general(head, full, by_rows, preferred_element_type=jnp.float32)
    high, low = two_part(gram)
    across = (jnp.dot(high, full, preferred_element_type=jnp.float32)
              + jnp.dot(low, full, preferred_element_type=jnp.float32))
    high, low = two_part(across)
    squared = (lax.dot_general(high, full, by_rows, preferred_element_type=jnp.float32)
               + lax.dot_general(low, full, by_rows, preferred_element_type=jnp.float32))
    poly = second_coef * gram + third_coef * squared
    high, low = two_part(poly)
    mixed = (jnp.dot(high, full, preferred_element_type=jnp.float32)
             + jnp.dot(low, full, preferred_element_type=jnp.float32))
    fresh = (first_coef * head.astype(jnp.float32) + mixed).astype(jnp.bfloat16)
    for j in range(n_tensor):
        piece_buf[j] = fresh[:, j * cols:(j + 1) * cols]
    pl.semaphore_wait(barrier, n_tensor - 1)
    own = pltpu.make_async_copy(piece_buf.at[t], out_buf.at[t], local_sem)
    own.start()
    copies = []
    for k in range(1, n_tensor):
        peer = lax.rem(t + k, n_tensor)
        copy = pltpu.make_async_remote_copy(
            src_ref=piece_buf.at[peer], dst_ref=out_buf.at[t],
            send_sem=send_sem.at[peer], recv_sem=recv_sem.at[t],
            device_id=here + (peer,), device_id_type=MESH)
        copy.start()
        copies.append(copy)
    own.wait()
    for k in range(1, n_tensor):
        peer = lax.rem(t + k, n_tensor)
        pltpu.make_async_remote_copy(
            src_ref=piece_buf.at[t], dst_ref=out_buf.at[peer],
            send_sem=send_sem.at[peer], recv_sem=recv_sem.at[peer],
            device_id=here + (peer,), device_id_type=MESH).wait_recv()
        copies[k - 1].wait_send()
    update = update_gain * math.sqrt(n_tensor * cols) * out_buf[...].astype(jnp.float32)
    update_ref[...] = update
    weight = weight_ref[...]
    weight_out[...] = weight - learn_rate * (update + weight_decay * weight)


def finish(iterate, weight, sizes, n_tensor, rows):
    cols = iterate.shape[1] // n_tensor
    shape = (n_tensor, rows, cols)
    vmem = pl.BlockSpec(memory_space=pltpu.VMEM)
    return pl.pallas_call(
        functools.partial(finish_kernel, sizes, n_tensor),
        out_shape=(jax.ShapeDtypeStruct(weight.shape, jnp.float32),
                   jax.ShapeDtypeStruct(weight.shape, jnp.float32)),
        in_specs=[vmem, vmem],
        out_specs=(vmem, vmem),
        scratch_shapes=[
            pltpu.VMEM(shape, iterate.dtype),
            pltpu.VMEM(shape, iterate.dtype),
            pltpu.SemaphoreType.DMA((n_tensor,)),
            pltpu.SemaphoreType.DMA((n_tensor,)),
            pltpu.SemaphoreType.DMA,
        ],
        compiler_params=pltpu.CompilerParams(collective_id=1, has_side_effects=True),
    )(iterate, weight)


def on_device(grad, momentum, weight):
    mats, rows_local, cols_local = grad.shape
    n_tensor = lax.axis_size("tensor")
    sizes = tuple(lax.axis_size(axis) for axis in SHARD_AXES)
    iterate, new_momentum = gather3(grad, momentum, sizes, n_tensor)
    block = 0
    for axis in reversed(SHARD_AXES):
        block = block * lax.axis_size(axis) + lax.axis_index(axis)
    start = block * rows_local

    def mine(full):
        return lax.dynamic_slice_in_dim(full, start, rows_local, axis=0)

    for step in range(ITERS - 1):
        gram = jnp.dot(iterate, iterate.T, preferred_element_type=jnp.float32)
        iterate = polish(iterate, gram)
    update, new_weight = finish(iterate, weight, sizes, n_tensor, rows_local)
    return (new_weight, new_momentum, update)


def split_shard(mesh):
    devices = mesh.devices
    column = devices[:, 0]
    try:
        n_x = len({d.coords[0] for d in column})
        n_z = len({d.coords[2] for d in column})
        n_core = len({d.core_on_chip for d in column})
    except AttributeError:
        n_x, n_z, n_core = len(column), 1, 1
    if n_x * n_z * n_core != len(column):
        n_x, n_z, n_core = len(column), 1, 1
    grid = devices.reshape(n_x, n_z, n_core, devices.shape[1])
    return jax.sharding.Mesh(grid, SHARD_AXES + ("tensor",))


def solution(mesh):
    fine = split_shard(mesh)
    spec = P(None, SHARD_AXES, "tensor")
    return jax.shard_map(
        on_device, mesh=fine, in_specs=(spec,) * 3, out_specs=(spec,) * 3, check_vma=False
    )
```

```python
import math

import jax
import jax.numpy as jnp
from jax import lax
from jax.experimental import pallas as pl
from jax.experimental.pallas import tpu as pltpu
from jax.sharding import PartitionSpec as P
import functools

ITERS = 3
SHARD_AXES = ("sx", "sz", "sc")


mu_decay = 0.95
learn_rate = 0.05
weight_decay = 0.1
update_gain = 0.2
first_coef = 3.4445
second_coef = -4.775
third_coef = 2.0315
epsilon = 1e-07


MESH = pl.DeviceIdType.MESH


def shard_coords(index, sizes):
    coords = []
    for size in reversed(sizes):
        coords.append(index % size)
        index = index // size
    return tuple(reversed(coords))


def gather3_kernel(sizes, n_tensor, grad_ref, momentum_ref, out_ref, momentum_out, gram_ref,
                   adv_ref, row_buf, whole_buf,
                   send1, recv1, send_x, recv_x, send_z, recv_z, send_c, recv_c, local_sem):
    mats, rows, cols = adv_ref.shape
    n_x, n_z, n_c = sizes
    x, z, c = (lax.axis_index(a) for a in SHARD_AXES)
    here = (x, z, c)
    t = lax.axis_index("tensor")

    def block(bx, bz, bc):
        return (bc * n_z + bz) * n_x + bx

    def span(first, count):
        return pl.ds(pl.multiple_of(first * rows, rows), count * rows)

    barrier = pltpu.get_barrier_semaphore()
    peers = [here + (lax.rem(t + k, n_tensor),) for k in range(1, n_tensor)]
    peers += [(lax.rem(x + k, n_x), z, c, t) for k in range(1, n_x)]
    peers += [(x, lax.rem(z + k, n_z), c, t) for k in range(1, n_z)]
    peers += [(x, z, lax.rem(c + k, n_c), t) for k in range(1, n_c)]
    for peer in peers:
        pl.semaphore_signal(barrier, inc=1, device_id=peer, device_id_type=MESH)
    fresh = mu_decay * momentum_ref[...] + grad_ref[...]
    momentum_out[...] = fresh
    adv_ref[...] = (grad_ref[...] + mu_decay * fresh).astype(adv_ref.dtype)
    pl.semaphore_wait(barrier, len(peers))

    my_cols = pl.ds(pl.multiple_of(t * cols, cols), cols)
    own = pltpu.make_async_copy(adv_ref.at[t], row_buf.at[:, my_cols], local_sem)
    own.start()
    sent = []
    for k in range(1, n_tensor):
        peer = lax.rem(t + k, n_tensor)
        copy = pltpu.make_async_remote_copy(
            src_ref=adv_ref.at[peer], dst_ref=row_buf.at[:, my_cols],
            send_sem=send1.at[peer], recv_sem=recv1.at[t],
            device_id=here + (peer,), device_id_type=MESH)
        copy.start()
        sent.append(copy)
    own.wait()
    for k in range(1, n_tensor):
        peer = lax.rem(t + k, n_tensor)
        peer_cols = pl.ds(pl.multiple_of(peer * cols, cols), cols)
        pltpu.make_async_remote_copy(
            src_ref=adv_ref.at[t], dst_ref=row_buf.at[:, peer_cols],
            send_sem=send1.at[peer], recv_sem=recv1.at[peer],
            device_id=here + (peer,), device_id_type=MESH).wait_recv()
    for copy in sent:
        copy.wait_send()

    mine = span(block(x, z, c), 1)
    own = pltpu.make_async_copy(row_buf, whole_buf.at[mine], local_sem)
    own.start()
    sent = []
    for k in range(1, n_x):
        peer = lax.rem(x + k, n_x)
        copy = pltpu.make_async_remote_copy(
            src_ref=row_buf, dst_ref=whole_buf.at[mine],
            send_sem=send_x.at[peer], recv_sem=recv_x.at[x],
            device_id=(peer, z, c, t), device_id_type=MESH)
        copy.start()
        sent.append(copy)
    own.wait()
    for k in range(1, n_x):
        peer = lax.rem(x + k, n_x)
        pltpu.make_async_remote_copy(
            src_ref=row_buf, dst_ref=whole_buf.at[span(block(peer, z, c), 1)],
            send_sem=send_x.at[peer], recv_sem=recv_x.at[peer],
            device_id=(peer, z, c, t), device_id_type=MESH).wait_recv()
    for copy in sent:
        copy.wait_send()

    strip = span(block(0, z, c), n_x)
    sent = []
    for k in range(1, n_z):
        peer = lax.rem(z + k, n_z)
        copy = pltpu.make_async_remote_copy(
            src_ref=whole_buf.at[strip], dst_ref=whole_buf.at[strip],
            send_sem=send_z.at[peer], recv_sem=recv_z.at[z],
            device_id=(x, peer, c, t), device_id_type=MESH)
        copy.start()
        sent.append(copy)
    for k in range(1, n_z):
        peer = lax.rem(z + k, n_z)
        other = span(block(0, peer, c), n_x)
        pltpu.make_async_remote_copy(
            src_ref=whole_buf.at[other], dst_ref=whole_buf.at[other],
            send_sem=send_z.at[peer], recv_sem=recv_z.at[peer],
            device_id=(x, peer, c, t), device_id_type=MESH).wait_recv()
    for copy in sent:
        copy.wait_send()

    half = span(block(0, 0, c), n_z * n_x)
    sent = []
    for k in range(1, n_c):
        peer = lax.rem(c + k, n_c)
        copy = pltpu.make_async_remote_copy(
            src_ref=whole_buf.at[half], dst_ref=whole_buf.at[half],
            send_sem=send_c.at[peer], recv_sem=recv_c.at[c],
            device_id=(x, z, peer, t), device_id_type=MESH)
        copy.start()
        sent.append(copy)
    for k in range(1, n_c):
        peer = lax.rem(c + k, n_c)
        other = span(block(0, 0, peer), n_z * n_x)
        pltpu.make_async_remote_copy(
            src_ref=whole_buf.at[other], dst_ref=whole_buf.at[other],
            send_sem=send_c.at[peer], recv_sem=recv_c.at[peer],
            device_id=(x, z, peer, t), device_id_type=MESH).wait_recv()
    for copy in sent:
        copy.wait_send()

    def square(i, total):
        piece = whole_buf[pl.ds(pl.multiple_of(i * rows, rows), rows), :].astype(jnp.float32)
        return total + piece * piece

    total = lax.fori_loop(0, n_x * n_z * n_c, square,
                          jnp.zeros((rows, n_tensor * cols), jnp.float32))
    frob = jnp.sqrt(jnp.sum(total, keepdims=True)) + epsilon

    def scale(i, carry):
        band = pl.ds(pl.multiple_of(i * rows, rows), rows)
        out_ref[band, :] = (whole_buf[band, :].astype(jnp.float32) / frob).astype(out_ref.dtype)
        return carry

    lax.fori_loop(0, n_x * n_z * n_c, scale, 0)
    start = out_ref[...]
    gram_ref[...] = lax.dot_general(start, start, (((1,), (1,)), ((), ())),
                                    preferred_element_type=jnp.float32)


def gather3(grad, momentum, sizes, n_tensor):
    mats, rows, cols = grad.shape
    n_x, n_z, n_c = sizes
    DMA = pltpu.SemaphoreType.DMA
    vmem = pl.BlockSpec(memory_space=pltpu.VMEM)
    return pl.pallas_call(
        functools.partial(gather3_kernel, sizes, n_tensor),
        out_shape=(
            jax.ShapeDtypeStruct((n_x * n_z * n_c * rows, n_tensor * cols), jnp.bfloat16),
            jax.ShapeDtypeStruct(momentum.shape, momentum.dtype),
            jax.ShapeDtypeStruct((n_x * n_z * n_c * rows,) * 2, jnp.float32),
        ),
        in_specs=[vmem, vmem],
        out_specs=(vmem, vmem, vmem),
        scratch_shapes=[
            pltpu.VMEM((mats, rows, cols), jnp.bfloat16),
            pltpu.VMEM((rows, n_tensor * cols), jnp.bfloat16),
            pltpu.VMEM((n_x * n_z * n_c * rows, n_tensor * cols), jnp.bfloat16),
            DMA((n_tensor,)), DMA((n_tensor,)),
            DMA((n_x,)), DMA((n_x,)),
            DMA((n_z,)), DMA((n_z,)),
            DMA((n_c,)), DMA((n_c,)),
            DMA,
        ],
        compiler_params=pltpu.CompilerParams(collective_id=0, has_side_effects=True),
    )(grad, momentum)


def scatter_kernel(n_tensor, piece_ref, out_ref, out_buf, send_sem, recv_sem, local_sem):
    here = tuple(lax.axis_index(a) for a in SHARD_AXES)
    t = lax.axis_index("tensor")
    barrier = pltpu.get_barrier_semaphore()
    for k in range(1, n_tensor):
        pl.semaphore_signal(barrier, inc=1, device_id=here + (lax.rem(t + k, n_tensor),),
                            device_id_type=MESH)
    pl.semaphore_wait(barrier, n_tensor - 1)
    own = pltpu.make_async_copy(piece_ref.at[t], out_buf.at[t], local_sem)
    own.start()
    copies = []
    for k in range(1, n_tensor):
        peer = lax.rem(t + k, n_tensor)
        copy = pltpu.make_async_remote_copy(
            src_ref=piece_ref.at[peer], dst_ref=out_buf.at[t],
            send_sem=send_sem.at[peer], recv_sem=recv_sem.at[t],
            device_id=here + (peer,), device_id_type=MESH)
        copy.start()
        copies.append(copy)
    own.wait()
    for k in range(1, n_tensor):
        peer = lax.rem(t + k, n_tensor)
        pltpu.make_async_remote_copy(
            src_ref=piece_ref.at[t], dst_ref=out_buf.at[peer],
            send_sem=send_sem.at[peer], recv_sem=recv_sem.at[peer],
            device_id=here + (peer,), device_id_type=MESH).wait_recv()
        copies[k - 1].wait_send()
    out_ref[...] = out_buf[...]


def scatter(pieces):
    n_tensor = pieces.shape[0]
    return pl.pallas_call(
        functools.partial(scatter_kernel, n_tensor),
        out_shape=jax.ShapeDtypeStruct(pieces.shape, pieces.dtype),
        in_specs=[pl.BlockSpec(memory_space=pltpu.VMEM)],
        out_specs=pl.BlockSpec(memory_space=pltpu.VMEM),
        scratch_shapes=[
            pltpu.VMEM(pieces.shape, pieces.dtype),
            pltpu.SemaphoreType.DMA((n_tensor,)),
            pltpu.SemaphoreType.DMA((n_tensor,)),
            pltpu.SemaphoreType.DMA,
        ],
        compiler_params=pltpu.CompilerParams(collective_id=1, has_side_effects=True),
    )(pieces)


def split_dot(wide_lhs, rhs):
    high = wide_lhs.astype(jnp.bfloat16)
    low = (wide_lhs - high.astype(jnp.float32)).astype(jnp.bfloat16)
    both = jnp.concatenate([high, low], axis=1)
    return jnp.dot(both, jnp.concatenate([rhs, rhs], axis=0), preferred_element_type=jnp.float32)


def polish(iterate, gram, rows=None):
    squared_rows = gram if rows is None else rows(gram)
    squared = jnp.dot(squared_rows, gram, precision=lax.Precision.HIGH)
    poly = second_coef * squared_rows + third_coef * squared
    head = iterate if rows is None else rows(iterate)
    fresh = first_coef * head.astype(jnp.float32) + split_dot(poly, iterate)
    return fresh.astype(jnp.bfloat16)


def two_part(wide):
    high = wide.astype(jnp.bfloat16)
    return high, (wide - high.astype(jnp.float32)).astype(jnp.bfloat16)


def finish_kernel(sizes, n_tensor, x_ref, out_ref, piece_buf, out_buf, send_sem, recv_sem, local_sem):
    n_x, n_z, n_c = sizes
    x, z, c = (lax.axis_index(a) for a in SHARD_AXES)
    here = (x, z, c)
    t = lax.axis_index("tensor")
    _, rows, cols = piece_buf.shape
    barrier = pltpu.get_barrier_semaphore()
    for k in range(1, n_tensor):
        pl.semaphore_signal(barrier, inc=1, device_id=here + (lax.rem(t + k, n_tensor),),
                            device_id_type=MESH)
    block = (c * n_z + z) * n_x + x
    head = x_ref[pl.ds(pl.multiple_of(block * rows, rows), rows), :]
    full = x_ref[...]
    by_rows = (((1,), (1,)), ((), ()))
    gram = lax.dot_general(head, full, by_rows, preferred_element_type=jnp.float32)
    high, low = two_part(gram)
    across = (jnp.dot(high, full, preferred_element_type=jnp.float32)
              + jnp.dot(low, full, preferred_element_type=jnp.float32))
    high, low = two_part(across)
    squared = (lax.dot_general(high, full, by_rows, preferred_element_type=jnp.float32)
               + lax.dot_general(low, full, by_rows, preferred_element_type=jnp.float32))
    poly = second_coef * gram + third_coef * squared
    high, low = two_part(poly)
    mixed = (jnp.dot(high, full, preferred_element_type=jnp.float32)
             + jnp.dot(low, full, preferred_element_type=jnp.float32))
    fresh = (first_coef * head.astype(jnp.float32) + mixed).astype(jnp.bfloat16)
    for j in range(n_tensor):
        piece_buf[j] = fresh[:, j * cols:(j + 1) * cols]
    pl.semaphore_wait(barrier, n_tensor - 1)
    own = pltpu.make_async_copy(piece_buf.at[t], out_buf.at[t], local_sem)
    own.start()
    copies = []
    for k in range(1, n_tensor):
        peer = lax.rem(t + k, n_tensor)
        copy = pltpu.make_async_remote_copy(
            src_ref=piece_buf.at[peer], dst_ref=out_buf.at[t],
            send_sem=send_sem.at[peer], recv_sem=recv_sem.at[t],
            device_id=here + (peer,), device_id_type=MESH)
        copy.start()
        copies.append(copy)
    own.wait()
    for k in range(1, n_tensor):
        peer = lax.rem(t + k, n_tensor)
        pltpu.make_async_remote_copy(
            src_ref=piece_buf.at[t], dst_ref=out_buf.at[peer],
            send_sem=send_sem.at[peer], recv_sem=recv_sem.at[peer],
            device_id=here + (peer,), device_id_type=MESH).wait_recv()
        copies[k - 1].wait_send()
    out_ref[...] = out_buf[...]


def finish(iterate, sizes, n_tensor, rows):
    cols = iterate.shape[1] // n_tensor
    shape = (n_tensor, rows, cols)
    return pl.pallas_call(
        functools.partial(finish_kernel, sizes, n_tensor),
        out_shape=jax.ShapeDtypeStruct(shape, iterate.dtype),
        in_specs=[pl.BlockSpec(memory_space=pltpu.VMEM)],
        out_specs=pl.BlockSpec(memory_space=pltpu.VMEM),
        scratch_shapes=[
            pltpu.VMEM(shape, iterate.dtype),
            pltpu.VMEM(shape, iterate.dtype),
            pltpu.SemaphoreType.DMA((n_tensor,)),
            pltpu.SemaphoreType.DMA((n_tensor,)),
            pltpu.SemaphoreType.DMA,
        ],
        compiler_params=pltpu.CompilerParams(collective_id=1, has_side_effects=True),
    )(iterate)


def on_device(grad, momentum, weight):
    mats, rows_local, cols_local = grad.shape
    n_tensor = lax.axis_size("tensor")
    sizes = tuple(lax.axis_size(axis) for axis in SHARD_AXES)
    iterate, new_momentum, gram = gather3(grad, momentum, sizes, n_tensor)
    block = 0
    for axis in reversed(SHARD_AXES):
        block = block * lax.axis_size(axis) + lax.axis_index(axis)
    start = block * rows_local

    def mine(full):
        return lax.dynamic_slice_in_dim(full, start, rows_local, axis=0)

    for step in range(ITERS - 1):
        if step:
            gram = jnp.dot(iterate, iterate.T, preferred_element_type=jnp.float32)
        iterate = polish(iterate, gram)
    ortho = finish(iterate, sizes, n_tensor, rows_local)
    width = cols_local * n_tensor
    update = update_gain * math.sqrt(width) * ortho.astype(jnp.float32)
    new_weight = weight - learn_rate * (update + weight_decay * weight)
    return (new_weight, new_momentum, update)


def split_shard(mesh):
    devices = mesh.devices
    column = devices[:, 0]
    try:
        n_x = len({d.coords[0] for d in column})
        n_z = len({d.coords[2] for d in column})
        n_core = len({d.core_on_chip for d in column})
    except AttributeError:
        n_x, n_z, n_core = len(column), 1, 1
    if n_x * n_z * n_core != len(column):
        n_x, n_z, n_core = len(column), 1, 1
    grid = devices.reshape(n_x, n_z, n_core, devices.shape[1])
    return jax.sharding.Mesh(grid, SHARD_AXES + ("tensor",))


def solution(mesh):
    fine = split_shard(mesh)
    spec = P(None, SHARD_AXES, "tensor")
    return jax.shard_map(
        on_device, mesh=fine, in_specs=(spec,) * 3, out_specs=(spec,) * 3, check_vma=False
    )
```
